32 devices in a mesh: seq: 16 (over z, y, core), head: 2 (over x).
Axes of the slice: x: 2, y: 2, z: 4, core: 2. Of those that a mesh axis runs over, the one named last changes fastest.
Arguments:
- queries: bfloat16 [8192, 4096], P(('seq', 'head')), may hold values from -64 to 64
- keys: bfloat16 [8192, 1024], P(('seq', 'head')), may hold values from -6 to 6
- values: bfloat16 [8192, 1024], P(('seq', 'head')), may hold values from -6 to 6
- level_bias: float32 [32, 4], P('head'), may hold values from -1 to 2
- anchor_bias: float32 [32], P('head'), may hold values from 1 to 4
- partners: int32 [16, 4], P('seq'), may hold values from 0 to 15, as said below
- anchor_positions: int32 [64], replicated, may hold values from 0 to 8191, as said below
Outputs:
- attended: bfloat16 [8192, 4096], P(('seq', 'head'))
The draws below stay inside these ranges and needn't reach their ends.
Inputs may be any that keep to these rules, and one draw needn't show every extreme that they name: `partners`: row b holds b XOR 2**j once for each j of 0 to 3, in an order drawn for each block. `anchor_positions`: distinct positions.
All inputs are finite; a program needn't handle non-finite values.
Results may differ from the reference program's by a relative error of at most 0.0045.
Values may be sent and summed in bfloat16 or wider, within the bound.
A program may use at most 192 MiB of HBM per device.

```python
import math
import jax
import jax.numpy as jnp
from jax import lax

QH = 32
KVH = 8
HD = 128
TOK_DEV = 512
NGLOB = 64
BLOCKS = 16
LEVELS = 4
TOKENS = 8192


def shared_keys(key):
    base_key = jax.random.fold_in(key, 7)
    drawn = jnp.clip(jax.random.normal(base_key, (TOKENS, KVH * HD), jnp.float32), -6.0, 6.0)
    return drawn


def draw_keys(key, part):
    drawn = shared_keys(key)
    return drawn.astype(jnp.bfloat16)


def draw_queries(key, part):
    noise_key = jax.random.fold_in(key, 13)
    result = jnp.clip(2.0 * jax.random.normal(noise_key, (TOKENS, QH * HD), jnp.float32), -8.0, 8.0)
    return result.astype(jnp.bfloat16)


def draw_partners(key, part):

    def one_block(block):
        order_bits = jax.random.permutation(jax.random.fold_in(key, block), LEVELS)
        return jnp.bitwise_xor(block, jnp.left_shift(1, order_bits)).astype(jnp.int32)
    return jax.vmap(one_block)(jnp.arange(BLOCKS, dtype=jnp.int32))


def draw_anchor_positions(key, part):
    return jax.random.permutation(jax.random.fold_in(key, 5), TOKENS)[:NGLOB].astype(jnp.int32)


def block_levels(stream_key, dims, split, smallest, largest):
    factor_of, own = 1.0, jax.random.fold_in(stream_key, 6)
    for axis_at, shards_of in split:
        draws = jnp.exp(jax.random.uniform(jax.random.fold_in(own, axis_at), (shards_of,), jnp.float32, smallest / len(split), largest / len(split)))
        factor_of = factor_of * jnp.repeat(draws, dims[axis_at] // shards_of).reshape([-1 if axis == axis_at else 1 for axis in range(len(dims))])
    return factor_of


def scatter_about(stream_key, extent, scale, most, split=(), kind=jnp.bfloat16):
    gain = block_levels(stream_key, extent, split, -0.22, 0.18) if split else 1.0
    values = jax.random.normal(stream_key, extent, jnp.float32) * scale * gain
    return jnp.minimum(jnp.maximum(values, -most), most).astype(kind)


def setup_inputs(seed: int = 0) -> dict:
    arg_keys = jax.random.split(jax.random.key(seed), 8)
    queries = draw_queries(jax.random.fold_in(arg_keys[7], 71), 0)
    keys = draw_keys(jax.random.fold_in(arg_keys[7], 71), 0)
    values = scatter_about(arg_keys[2], (TOKENS, KVH * HD), 1.0, 6.0, ((0, 32),))
    level_bias = jnp.clip(-1.0 + 3.0 * jax.random.uniform(arg_keys[3], (QH, LEVELS), jnp.float32) ** block_levels(arg_keys[3], (QH, LEVELS), ((0, 2),), -0.2, 0.2), -1.0, 2.0)
    anchor_bias = jnp.clip(jnp.exp(math.log(4.0) - 1.3862944 * jax.random.uniform(arg_keys[4], (QH,), jnp.float32) ** block_levels(arg_keys[4], (QH,), ((0, 2),), -0.2, 0.2)), 1.0, 4.0)
    partners = draw_partners(jax.random.fold_in(arg_keys[7], 71), 0)
    anchor_positions = draw_anchor_positions(jax.random.fold_in(arg_keys[7], 71), 0)
    return dict(queries=queries, keys=keys, values=values, level_bias=level_bias, anchor_bias=anchor_bias, partners=partners, anchor_positions=anchor_positions)


def reference(queries, keys, values, level_bias, anchor_bias, partners, anchor_positions):
    group_size = QH // KVH
    score_scale = HD ** -0.5
    anchor_keys = keys[anchor_positions]
    anchor_vals = values[anchor_positions]
    pieces = [jnp.zeros((QH, TOK_DEV), jnp.float32)]
    for level in range(LEVELS):
        pieces.append(jnp.broadcast_to(level_bias[:, level:level + 1], (QH, TOK_DEV)))
    pieces.append(jnp.broadcast_to(anchor_bias[:, None], (QH, NGLOB)))
    key_bias = jnp.concatenate(pieces, axis=1).reshape(KVH, group_size, -1)

    def attend_block(block):
        start = (block * TOK_DEV).astype(jnp.int32)
        query_heads = lax.dynamic_slice_in_dim(queries, start, TOK_DEV, 0).reshape(TOK_DEV, KVH, group_size, HD)
        key_list = [lax.dynamic_slice_in_dim(keys, start, TOK_DEV, 0)]
        value_list = [lax.dynamic_slice_in_dim(values, start, TOK_DEV, 0)]
        for level in range(LEVELS):
            other = (partners[block, level] * TOK_DEV).astype(jnp.int32)
            key_list.append(lax.dynamic_slice_in_dim(keys, other, TOK_DEV, 0))
            value_list.append(lax.dynamic_slice_in_dim(values, other, TOK_DEV, 0))
        key_rows = jnp.concatenate(key_list + [anchor_keys], axis=0).reshape(-1, KVH, HD)
        value_rows = jnp.concatenate(value_list + [anchor_vals], axis=0).reshape(-1, KVH, HD)
        scores = jnp.einsum("tkgd,skd->kgts", query_heads.astype(jnp.float32), key_rows.astype(jnp.float32))
        scores = scores * score_scale + key_bias[:, :, None, :]
        row_max = jnp.max(scores, axis=-1, keepdims=True)
        weights = jnp.exp(scores - row_max)
        denominator = jnp.sum(weights, axis=-1)
        rounded = lax.optimization_barrier(weights.astype(jnp.bfloat16)).astype(jnp.float32)
        numerator = jnp.einsum("kgts,skd->kgtd", rounded, value_rows.astype(jnp.float32))
        result = numerator / denominator[..., None]
        return result.transpose(2, 0, 1, 3).reshape(TOK_DEV, QH * HD).astype(jnp.bfloat16)

    blocks_out = lax.map(attend_block, jnp.arange(BLOCKS, dtype=jnp.int32))
    return blocks_out.reshape(TOKENS, QH * HD)
```

```python
import functools

import jax
import jax.numpy as jnp
from jax import lax
from jax.experimental import pallas as pl
from jax.experimental.pallas import tpu as pltpu
from jax.sharding import PartitionSpec as P

HD = 128
LOG2E = 1.4426950408889634


def attend(query, key_parts, value_parts, biases, scale):
    scores = [
        lax.dot_general(query, k, (((1,), (1,)), ((), ())), preferred_element_type=jnp.float32)
        for k in key_parts
    ]
    row_max = None
    for s, b in zip(scores, biases):
        top = jnp.max(s, axis=1, keepdims=True) * scale + b
        row_max = top if row_max is None else jnp.maximum(row_max, top)
    total = None
    acc = None
    for s, v, b in zip(scores, value_parts, biases):
        p = jnp.exp2(s * scale + (b - row_max))
        part = jnp.sum(p, axis=1, keepdims=True)
        out = jnp.dot(p.astype(jnp.bfloat16), v, preferred_element_type=jnp.float32)
        total = part if total is None else total + part
        acc = out if acc is None else acc + out
    return acc / total


def kernel(
    heads, levels, kv_local, group,
    level_ref, anchor_ref, partners_ref, places_ref, keys_ref, values_ref, queries_ref, out_ref,
    kv, qbuf, obuf, full, part, part_in, head_out, head_in, carry, carry_in, table,
    own_sem, full_sem, own_q_sem, own_o_sem,
    x_send, x_recv, q_send, q_recv, o_send, o_recv, lv_send, lv_recv,
    core_send, core_recv, head_send, head_recv, carry_send, carry_recv,
    last_sem, last_send, last_recv,
):
    me = lax.axis_index("head")
    seat = lax.axis_index("seq")
    t = keys_ref.shape[0]
    block = heads * t
    wide = group * HD
    anchors = places_ref.shape[1]
    scale = HD ** -0.5 * LOG2E
    mesh_id = pl.DeviceIdType.MESH
    bf16 = jnp.bfloat16
    sources = (keys_ref, values_ref)
    mine = lax.rem(seat, 2)

    def peer(d):
        return lax.rem(me + d, heads)

    def partner(l):
        bit = lax.rem(lax.div(seat, 1 << l), 2)
        return seat + (1 - 2 * bit) * (1 << l)

    def cols(owner, j, width):
        return pl.ds(pl.multiple_of((owner * kv_local + j) * width, width), width)

    def rows(n, r):
        return pl.ds(pl.multiple_of(n * block + r * t, t), t)

    anchor_rows = pl.ds((levels + 1) * block, anchors)

    def to_head(src, dst, send, recv, d):
        return pltpu.make_async_remote_copy(
            src_ref=src, dst_ref=dst, send_sem=send, recv_sem=recv,
            device_id={"head": peer(d)}, device_id_type=mesh_id)

    def to_level(src, dst, send, recv, l):
        return pltpu.make_async_remote_copy(
            src_ref=src, dst_ref=dst, send_sem=send, recv_sem=recv,
            device_id={"seq": partner(l)}, device_id_type=mesh_id)

    def own_copy(j, c):
        return pltpu.make_async_copy(
            sources[c].at[:, cols(me, j, HD)], kv.at[j, c, rows(0, me)], own_sem.at[j, c])

    def full_copy(c):
        return pltpu.make_async_copy(sources[c], full.at[c], full_sem.at[c])

    def own_q(j):
        return pltpu.make_async_copy(
            queries_ref.at[:, cols(me, j, wide)], qbuf.at[j, 0], own_q_sem.at[j])

    def send_kv(j, c, d):
        return to_head(
            sources[c].at[:, cols(peer(d), j, HD)], kv.at[j, c, rows(0, me)],
            x_send.at[j, c, d], x_recv.at[j, c, d], d)

    def came_kv(j, c, d):
        return to_head(
            sources[c].at[:, cols(me, j, HD)], kv.at[j, c, rows(0, peer(heads - d))],
            x_send.at[j, c, d], x_recv.at[j, c, d], d)

    def send_q(j, d):
        return to_head(
            queries_ref.at[:, cols(peer(d), j, wide)], qbuf.at[j, d],
            q_send.at[j, d], q_recv.at[j, d], d)

    def send_level(j, c, d, l):
        r = peer(heads - d)
        src = sources[c].at[:, cols(me, j, HD)] if d == 0 else kv.at[j, c, rows(0, r)]
        return to_level(
            src, kv.at[j, c, rows(l + 1, r)],
            lv_send.at[j, c, d, l], lv_recv.at[j, c, d, l], l)

    def level_came(j, c, d, l):
        r = peer(heads - d)
        return to_level(
            kv.at[j, c, rows(0, r)], kv.at[j, c, rows(l + 1, r)],
            lv_send.at[j, c, d, l], lv_recv.at[j, c, d, l], l)

    def send_core():
        return to_level(part.at[1 - mine], part_in, core_send, core_recv, 0)

    def send_part(d):
        return to_head(head_out.at[d], head_in.at[d], head_send.at[d], head_recv.at[d], d)

    def send_carry(i, l):
        return to_level(carry.at[i], carry_in.at[i], carry_send.at[i], carry_recv.at[i], l)

    def own_last(j):
        return pltpu.make_async_copy(
            carry.at[levels - 1, j], kv.at[j, mine, anchor_rows], last_sem.at[j])

    def send_last(j):
        return to_level(
            carry.at[levels - 1, j], kv.at[j, mine, anchor_rows],
            last_send.at[j], last_recv.at[j], 0)

    def last_came(j):
        return to_level(
            carry.at[levels - 1, j], kv.at[j, 1 - mine, anchor_rows],
            last_send.at[j], last_recv.at[j], 0)

    def out_cols(owner, j, g):
        return pl.ds(pl.multiple_of(((owner * kv_local + j) * group + g) * HD, HD), HD)

    def send_out(j, g, d):
        return to_head(
            obuf.at[j, d, g], out_ref.at[:, out_cols(me, j, g)],
            o_send.at[j, g, d], o_recv.at[j, g, d], heads - d)

    def came_out(j, g, d):
        return to_head(
            obuf.at[j, d, g], out_ref.at[:, out_cols(peer(d), j, g)],
            o_send.at[j, g, d], o_recv.at[j, g, d], heads - d)

    def own_out(j, g):
        return pltpu.make_async_copy(
            obuf.at[j, 0, g], out_ref.at[:, out_cols(me, j, g)], own_o_sem.at[j, g])

    barrier = pltpu.get_barrier_semaphore()
    for d in range(1, heads):
        pl.semaphore_signal(barrier, inc=1, device_id={"head": peer(d)}, device_id_type=mesh_id)
    for l in range(levels):
        pl.semaphore_signal(barrier, inc=1, device_id={"seq": partner(l)}, device_id_type=mesh_id)

    for c in range(2):
        full_copy(c).start()
    for j in range(kv_local):
        for c in range(2):
            own_copy(j, c).start()
    pl.semaphore_wait(barrier, heads - 1 + levels)

    far = list(reversed(range(levels)))

    def push_kv(j):
        for d in range(1, heads):
            for c in range(2):
                send_kv(j, c, d).start()

    def push_levels(j, c, d):
        for l in far:
            send_level(j, c, d, l).start()

    push_kv(0)
    for c in range(2):
        push_levels(0, c, 0)

    first = (seat * heads + me) * t
    places = places_ref[...] - first
    token = lax.broadcasted_iota(jnp.int32, (t, anchors), 0)
    selector = jnp.where(places == token, 1.0, 0.0).astype(bf16)
    for c in range(2):
        full_copy(c).wait()
        for d in range(heads):
            for j in range(kv_local):
                part[c, d, j] = lax.dot_general(
                    selector, full[c, :, cols(peer(d), j, HD)], (((0,), (0,)), ((), ())),
                    preferred_element_type=jnp.float32).astype(bf16)
    send_core().start()
    send_core().wait_recv()
    for d in range(heads):
        head_out[d] = (
            part[mine, d].astype(jnp.float32) + part_in[d].astype(jnp.float32)).astype(bf16)
    for d in range(1, heads):
        send_part(d).start()
    for j in range(1, kv_local):
        push_kv(j)
    for j in range(kv_local):
        for d in range(1, heads):
            send_q(j, d).start()
        own_q(j).start()

    def wait_kv(j, c):
        own_copy(j, c).wait()
        for d in range(1, heads):
            came_kv(j, c, d).wait_recv()

    pending = [(0, c, d) for c in range(2) for d in range(1, heads)]
    for j in range(1, kv_local):
        pending += [(j, c, 0) for c in range(2)]
        pending += [(j, c, d) for c in range(2) for d in range(1, heads)]

    def push(count):
        for _ in range(min(count, len(pending))):
            j, c, d = pending.pop(0)
            if d == 0:
                own_copy(j, c).wait()
            else:
                came_kv(j, c, d).wait_recv()
            push_levels(j, c, d)

    for c in range(2):
        own_copy(0, c).wait()

    def fill(h, _):
        for l in range(levels):
            total = jnp.float32(0.0)
            for m in range(levels):
                total += jnp.where(partners_ref[0, m] == partner(l), level_ref[m, h], 0.0)
            table[l, h] = total * LOG2E
        table[levels, h] = anchor_ref[h] * LOG2E
        return 0

    lax.fori_loop(0, kv_local * group, fill, 0)

    held = head_out[0].astype(jnp.float32)
    for d in range(1, heads):
        send_part(d).wait_recv()
        held = held + head_in[d].astype(jnp.float32)
    carry[0] = held.astype(bf16)
    order = list(range(2, levels)) + ([1] if levels > 1 else [])
    for i, l in enumerate(order):
        send_carry(i, l).start()
        push(1)
        send_carry(i, l).wait_recv()
        carry[i + 1] = (
            carry[i].astype(jnp.float32) + carry_in[i].astype(jnp.float32)).astype(bf16)
    for j in range(kv_local):
        own_last(j).start()
        send_last(j).start()
    push(len(pending))

    def one(step, _):
        j = lax.div(step, heads)
        turn = lax.rem(step, heads)

        @pl.when(turn == 0)
        def _():
            own_last(j).wait()
            last_came(j).wait_recv()
            for l in range(levels):
                for c in range(2):
                    for d in range(heads):
                        level_came(j, c, d, l).wait_recv()

        d = lax.rem(turn + 1, heads)

        @pl.when(turn < heads - 1)
        def _():
            send_q(j, d).wait_recv()

        @pl.when(turn == heads - 1)
        def _():
            own_q(j).wait()

        for g in range(group):
            h = j * group + g
            result = attend(
                qbuf[j, d, :, g * HD:(g + 1) * HD],
                [kv[j, 0, n * block:(n + 1) * block] for n in range(levels + 1)]
                + [kv[j, 0, (levels + 1) * block:]],
                [kv[j, 1, n * block:(n + 1) * block] for n in range(levels + 1)]
                + [kv[j, 1, (levels + 1) * block:]],
                [jnp.float32(0.0)] + [table[l, h] for l in range(levels + 1)],
                scale,
            )
            obuf[j, d, g] = result.astype(bf16)

            @pl.when(turn < heads - 1)
            def _():
                send_out(j, g, d).start()

            @pl.when(turn == heads - 1)
            def _():
                own_out(j, g).start()

        return 0

    lax.fori_loop(0, kv_local * heads, one, 0)

    send_core().wait_send()
    for d in range(1, heads):
        send_part(d).wait_send()
    for i, l in enumerate(order):
        send_carry(i, l).wait_send()
    for j in range(kv_local):
        send_last(j).wait_send()
        for c in range(2):
            for d in range(heads):
                for l in range(levels):
                    send_level(j, c, d, l).wait_send()
            for d in range(1, heads):
                send_kv(j, c, d).wait_send()
        for d in range(1, heads):
            send_q(j, d).wait_send()
        for g in range(group):
            own_out(j, g).wait()
            for d in range(1, heads):
                send_out(j, g, d).wait_send()
                came_out(j, g, d).wait_recv()


def on_device(queries, keys, values, level_bias, anchor_bias, partners, anchor_positions):
    t = queries.shape[0]
    heads = lax.axis_size("head")
    levels = lax.axis_size("seq").bit_length() - 1
    kv_local = keys.shape[1] // HD // heads
    group = level_bias.shape[0] // kv_local
    anchors = anchor_positions.shape[0]
    smem = pl.BlockSpec(memory_space=pltpu.SMEM)
    vmem = pl.BlockSpec(memory_space=pltpu.VMEM)
    hbm = pl.BlockSpec(memory_space=pl.ANY)
    dma = pltpu.SemaphoreType.DMA
    anchor_shape = (kv_local, anchors, HD)
    bf16 = jnp.bfloat16
    return pl.pallas_call(
        functools.partial(kernel, heads, levels, kv_local, group),
        in_specs=[smem, smem, smem, vmem, hbm, hbm, hbm],
        out_specs=hbm,
        out_shape=jax.ShapeDtypeStruct(queries.shape, queries.dtype),
        scratch_shapes=[
            pltpu.VMEM((kv_local, 2, (levels + 1) * heads * t + anchors, HD), bf16),
            pltpu.VMEM((kv_local, heads, t, group * HD), bf16),
            pltpu.VMEM((kv_local, heads, group, t, HD), bf16),
            pltpu.VMEM((2,) + keys.shape, bf16),
            pltpu.VMEM((2, heads) + anchor_shape, bf16),
            pltpu.VMEM((heads,) + anchor_shape, bf16),
            pltpu.VMEM((heads,) + anchor_shape, bf16),
            pltpu.VMEM((heads,) + anchor_shape, bf16),
            pltpu.VMEM((levels,) + anchor_shape, bf16),
            pltpu.VMEM((levels,) + anchor_shape, bf16),
            pltpu.SMEM((levels + 1, kv_local * group), jnp.float32),
            dma((kv_local, 2)), dma((2,)), dma((kv_local,)), dma((kv_local, group)),
            dma((kv_local, 2, heads)), dma((kv_local, 2, heads)),
            dma((kv_local, heads)), dma((kv_local, heads)),
            dma((kv_local, group, heads)), dma((kv_local, group, heads)),
            dma((kv_local, 2, heads, levels)), dma((kv_local, 2, heads, levels)),
            dma, dma, dma((heads,)), dma((heads,)), dma((levels,)), dma((levels,)),
            dma((kv_local,)), dma((kv_local,)), dma((kv_local,)),
        ],
        compiler_params=pltpu.CompilerParams(collective_id=0, has_side_effects=True),
        name="attend",
    )(level_bias.T, anchor_bias, partners, anchor_positions[None, :], keys, values, queries)


def solution(mesh):
    in_specs = (
        P(("seq", "head"), None),
        P(("seq", "head"), None),
        P(("seq", "head"), None),
        P("head", None),
        P("head"),
        P("seq", None),
        P(),
    )
    out_specs = P(("seq", "head"), None)
    return jax.shard_map(
        on_device, mesh=mesh, in_specs=in_specs, out_specs=out_specs, check_vma=False
    )
```

```python
import functools

import jax
import jax.numpy as jnp
from jax import lax
from jax.experimental import pallas as pl
from jax.experimental.pallas import tpu as pltpu
from jax.sharding import PartitionSpec as P

HD = 128
LOG2E = 1.4426950408889634


def attend(query, keys, values, biases, scale):
    scaled = query.astype(jnp.float32) * scale
    high = scaled.astype(jnp.bfloat16)
    low = (scaled - high.astype(jnp.float32)).astype(jnp.bfloat16)
    query = jnp.concatenate([high, low], axis=1)
    scores = [
        lax.dot_general(
            query, jnp.concatenate([k, k], axis=1), (((1,), (1,)), ((), ())),
            preferred_element_type=jnp.float32)
        for k in keys
    ]
    row_max = None
    for s, b in zip(scores, biases):
        top = jnp.max(s, axis=1, keepdims=True) + b
        row_max = top if row_max is None else jnp.maximum(row_max, top)
    weights = jnp.concatenate(
        [jnp.exp2(s - (row_max - b)).astype(jnp.bfloat16) for s, b in zip(scores, biases)], axis=1)
    both = jnp.dot(
        weights, jnp.concatenate([values, jnp.ones_like(values)], axis=1),
        preferred_element_type=jnp.float32)
    return both[:, :HD] / both[:, HD:]


def kernel(
    heads, levels, kv_local, group,
    level_hbm, anchor_hbm, partners_hbm, places_hbm, keys_ref, values_ref, queries_ref, out_ref,
    level_ref, anchor_ref, partners_ref, places_ref, small_sem,
    kv, qbuf, obuf, full, part, part_in, head_out, head_in, carry, carry_in, table,
    own_sem, full_sem, own_q_sem,
    x_send, x_recv, q_send, q_recv, o_send, o_recv, lv_send, lv_recv,
    core_send, core_recv, head_send, head_recv, carry_send, carry_recv,
    last_sem, last_send, last_recv,
):
    me = lax.axis_index("head")
    seat = lax.axis_index("seq")
    t = keys_ref.shape[0]
    block = heads * t
    wide = group * HD
    anchors = places_ref.shape[1]
    scale = HD ** -0.5 * LOG2E
    mesh_id = pl.DeviceIdType.MESH
    bf16 = jnp.bfloat16
    sources = (keys_ref, values_ref)
    mine = lax.rem(seat, 2)

    def peer(d):
        return lax.rem(me + d, heads)

    def partner(l):
        bit = lax.rem(lax.div(seat, 1 << l), 2)
        return seat + (1 - 2 * bit) * (1 << l)

    def cols(owner, j, width):
        return pl.ds(pl.multiple_of((owner * kv_local + j) * width, width), width)

    def rows(n, r):
        return pl.ds(pl.multiple_of(n * block + r * t, t), t)

    anchor_rows = pl.ds((levels + 1) * block, anchors)

    def to_head(src, dst, send, recv, d):
        return pltpu.make_async_remote_copy(
            src_ref=src, dst_ref=dst, send_sem=send, recv_sem=recv,
            device_id={"head": peer(d)}, device_id_type=mesh_id)

    def to_level(src, dst, send, recv, l):
        return pltpu.make_async_remote_copy(
            src_ref=src, dst_ref=dst, send_sem=send, recv_sem=recv,
            device_id={"seq": partner(l)}, device_id_type=mesh_id)

    def own_copy(j, c):
        return pltpu.make_async_copy(
            sources[c].at[:, cols(me, j, HD)], kv.at[j, c, rows(0, me)], own_sem.at[j, c])

    def full_copy(c):
        return pltpu.make_async_copy(sources[c], full.at[c], full_sem.at[c])

    def own_q(j):
        return pltpu.make_async_copy(
            queries_ref.at[:, cols(me, j, wide)], qbuf.at[j, 0], own_q_sem.at[j])

    def send_kv(j, c, d):
        return to_head(
            sources[c].at[:, cols(peer(d), j, HD)], kv.at[j, c, rows(0, me)],
            x_send.at[j, c, d], x_recv.at[j, c, d], d)

    def came_kv(j, c, d):
        return to_head(
            sources[c].at[:, cols(me, j, HD)], kv.at[j, c, rows(0, peer(heads - d))],
            x_send.at[j, c, d], x_recv.at[j, c, d], d)

    def send_q(j, d):
        return to_head(
            queries_ref.at[:, cols(peer(d), j, wide)], qbuf.at[j, d],
            q_send.at[j, d], q_recv.at[j, d], d)

    def send_level(j, c, d, l):
        r = peer(heads - d)
        src = sources[c].at[:, cols(me, j, HD)] if d == 0 else kv.at[j, c, rows(0, r)]
        return to_level(
            src, kv.at[j, c, rows(l + 1, r)],
            lv_send.at[j, c, d, l], lv_recv.at[j, c, d, l], l)

    def level_came(j, c, d, l):
        r = peer(heads - d)
        return to_level(
            kv.at[j, c, rows(0, r)], kv.at[j, c, rows(l + 1, r)],
            lv_send.at[j, c, d, l], lv_recv.at[j, c, d, l], l)

    def send_core():
        return to_level(part.at[1 - mine], part_in, core_send, core_recv, 0)

    def send_part(d):
        return to_head(head_out.at[d], head_in.at[d], head_send.at[d], head_recv.at[d], d)

    def send_carry(i, l):
        return to_level(carry.at[i], carry_in.at[i], carry_send.at[i], carry_recv.at[i], l)

    def own_last(j):
        return pltpu.make_async_copy(
            carry.at[levels - 1, j], kv.at[j, mine, anchor_rows], last_sem.at[j])

    def send_last(j):
        return to_level(
            carry.at[levels - 1, j], kv.at[j, mine, anchor_rows],
            last_send.at[j], last_recv.at[j], 0)

    def last_came(j):
        return to_level(
            carry.at[levels - 1, j], kv.at[j, 1 - mine, anchor_rows],
            last_send.at[j], last_recv.at[j], 0)

    def out_cols(owner, j, g):
        return pl.ds(pl.multiple_of(((owner * kv_local + j) * group + g) * HD, HD), HD)

    def send_out(j, g, d):
        return to_head(
            obuf.at[j, d, g], out_ref.at[:, out_cols(me, j, g)],
            o_send.at[j, g, d], o_recv.at[j, g, d], heads - d)

    def came_out(j, g, d):
        return to_head(
            obuf.at[j, d, g], out_ref.at[:, out_cols(peer(d), j, g)],
            o_send.at[j, g, d], o_recv.at[j, g, d], heads - d)

    def small(i):
        src = (level_hbm, anchor_hbm, partners_hbm, places_hbm)[i]
        dst = (level_ref, anchor_ref, partners_ref, places_ref)[i]
        return pltpu.make_async_copy(src, dst, small_sem.at[i])

    barrier = pltpu.get_barrier_semaphore()
    for d in range(1, heads):
        pl.semaphore_signal(barrier, inc=1, device_id={"head": peer(d)}, device_id_type=mesh_id)
    for l in range(levels):
        pl.semaphore_signal(barrier, inc=1, device_id={"seq": partner(l)}, device_id_type=mesh_id)

    for c in range(2):
        full_copy(c).start()
    for i in range(4):
        small(i).start()
    for j in range(kv_local):
        for c in range(2):
            own_copy(j, c).start()
        own_q(j).start()
    pl.semaphore_wait(barrier, heads - 1 + levels)

    far = list(reversed(range(levels)))

    def push_kv(j):
        for d in range(1, heads):
            for c in range(2):
                send_kv(j, c, d).start()

    def push_levels(j, c, d):
        for l in far:
            send_level(j, c, d, l).start()

    push_kv(0)
    for c in range(2):
        push_levels(0, c, 0)

    small(3).wait()
    first = (seat * heads + me) * t
    places = places_ref[...] - first
    token = lax.broadcasted_iota(jnp.int32, (t, anchors), 0)
    selector = jnp.where(places == token, 1.0, 0.0).astype(bf16)
    for c in range(2):
        full_copy(c).wait()
        for d in range(heads):
            for j in range(kv_local):
                part[c, d, j] = lax.dot_general(
                    selector, full[c, :, cols(peer(d), j, HD)], (((0,), (0,)), ((), ())),
                    preferred_element_type=jnp.float32).astype(bf16)
    send_core().start()
    send_core().wait_recv()
    for d in range(heads):
        head_out[d] = (
            part[mine, d].astype(jnp.float32) + part_in[d].astype(jnp.float32)).astype(bf16)
    for d in range(1, heads):
        send_part(d).start()
    for j in range(1, kv_local):
        push_kv(j)
    for j in range(kv_local):
        for d in range(1, heads):
            send_q(j, d).start()

    def wait_kv(j, c):
        own_copy(j, c).wait()
        for d in range(1, heads):
            came_kv(j, c, d).wait_recv()

    pending = [(0, c, d) for c in range(2) for d in range(1, heads)]
    for j in range(1, kv_local):
        pending += [(j, c, 0) for c in range(2)]
        pending += [(j, c, d) for c in range(2) for d in range(1, heads)]

    def push(count):
        for _ in range(min(count, len(pending))):
            j, c, d = pending.pop(0)
            if d == 0:
                own_copy(j, c).wait()
            else:
                came_kv(j, c, d).wait_recv()
            push_levels(j, c, d)

    for c in range(2):
        own_copy(0, c).wait()

    for i in range(3):
        small(i).wait()

    def fill(h, _):
        for l in range(levels):
            total = jnp.float32(0.0)
            for m in range(levels):
                total += jnp.where(partners_ref[0, m] == partner(l), level_ref[m, h], 0.0)
            table[l, h] = total * LOG2E
        table[levels, h] = anchor_ref[h] * LOG2E
        return 0

    lax.fori_loop(0, kv_local * group, fill, 0)

    held = head_out[0].astype(jnp.float32)
    for d in range(1, heads):
        send_part(d).wait_recv()
        held = held + head_in[d].astype(jnp.float32)
    carry[0] = held.astype(bf16)
    order = list(range(2, levels)) + ([1] if levels > 1 else [])
    for i, l in enumerate(order):
        send_carry(i, l).start()
        push(1)
        send_carry(i, l).wait_recv()
        carry[i + 1] = (
            carry[i].astype(jnp.float32) + carry_in[i].astype(jnp.float32)).astype(bf16)
    for j in range(kv_local):
        own_last(j).start()
        send_last(j).start()
    push(len(pending))

    def answer(j, d, g):
        return attend(
            qbuf[j, d, :, g * HD:(g + 1) * HD],
            [kv[j, 0, n * block:(n + 1) * block] for n in range(levels + 1)]
            + [kv[j, 0, (levels + 1) * block:]],
            kv[j, 1],
            [jnp.float32(0.0)] + [table[l, j * group + g] for l in range(levels + 1)],
            scale,
        ).astype(bf16)

    def one(j, _):
        own_last(j).wait()
        last_came(j).wait_recv()
        for l in range(levels):
            for c in range(2):
                for d in range(heads):
                    level_came(j, c, d, l).wait_recv()

        def remote(i, _):
            d = i + 1
            send_q(j, d).wait_recv()
            for g in range(group):
                obuf[j, d, g] = answer(j, d, g)
                send_out(j, g, d).start()
            return 0

        lax.fori_loop(0, heads - 1, remote, 0)
        own_q(j).wait()
        for g in range(group):
            out_ref[:, out_cols(me, j, g)] = answer(j, 0, g)
        return 0

    lax.fori_loop(0, kv_local, one, 0)

    send_core().wait_send()
    for d in range(1, heads):
        send_part(d).wait_send()
    for i, l in enumerate(order):
        send_carry(i, l).wait_send()
    for j in range(kv_local):
        send_last(j).wait_send()
        for c in range(2):
            for d in range(heads):
                for l in range(levels):
                    send_level(j, c, d, l).wait_send()
            for d in range(1, heads):
                send_kv(j, c, d).wait_send()
        for d in range(1, heads):
            send_q(j, d).wait_send()
        for g in range(group):
            for d in range(1, heads):
                send_out(j, g, d).wait_send()
                came_out(j, g, d).wait_recv()


def on_device(queries, keys, values, level_bias, anchor_bias, partners, anchor_positions):
    t = queries.shape[0]
    heads = lax.axis_size("head")
    levels = lax.axis_size("seq").bit_length() - 1
    kv_local = keys.shape[1] // HD // heads
    group = level_bias.shape[0] // kv_local
    anchors = anchor_positions.shape[0]
    vmem = pl.BlockSpec(memory_space=pltpu.VMEM)
    hbm = pl.BlockSpec(memory_space=pl.ANY)
    dma = pltpu.SemaphoreType.DMA
    anchor_shape = (kv_local, anchors, HD)
    bf16 = jnp.bfloat16
    grant = (61 << 20) - 500_000 - queries.size * queries.dtype.itemsize
    return pl.pallas_call(
        functools.partial(kernel, heads, levels, kv_local, group),
        in_specs=[hbm] * 7,
        out_specs=vmem,
        out_shape=pltpu.VMEM(queries.shape, queries.dtype),
        scratch_shapes=[
            pltpu.SMEM(level_bias.shape[::-1], level_bias.dtype),
            pltpu.SMEM(anchor_bias.shape, anchor_bias.dtype),
            pltpu.SMEM(partners.shape, partners.dtype),
            pltpu.VMEM((1, anchors), anchor_positions.dtype),
            dma((4,)),
            pltpu.VMEM((kv_local, 2, (levels + 1) * heads * t + anchors, HD), bf16),
            pltpu.VMEM((kv_local, heads, t, group * HD), bf16),
            pltpu.VMEM((kv_local, heads, group, t, HD), bf16),
            pltpu.VMEM((2,) + keys.shape, bf16),
            pltpu.VMEM((2, heads) + anchor_shape, bf16),
            pltpu.VMEM((heads,) + anchor_shape, bf16),
            pltpu.VMEM((heads,) + anchor_shape, bf16),
            pltpu.VMEM((heads,) + anchor_shape, bf16),
            pltpu.VMEM((levels,) + anchor_shape, bf16),
            pltpu.VMEM((levels,) + anchor_shape, bf16),
            pltpu.SMEM((levels + 1, kv_local * group), jnp.float32),
            dma((kv_local, 2)), dma((2,)), dma((kv_local,)),
            dma((kv_local, 2, heads)), dma((kv_local, 2, heads)),
            dma((kv_local, heads)), dma((kv_local, heads)),
            dma((kv_local, group, heads)), dma((kv_local, group, heads)),
            dma((kv_local, 2, heads, levels)), dma((kv_local, 2, heads, levels)),
            dma, dma, dma((heads,)), dma((heads,)), dma((levels,)), dma((levels,)),
            dma((kv_local,)), dma((kv_local,)), dma((kv_local,)),
        ],
        compiler_params=pltpu.CompilerParams(
            vmem_limit_bytes=grant, collective_id=0, has_side_effects=True),
        name="attend",
    )(level_bias.T, anchor_bias, partners, anchor_positions[None, :], keys, values, queries)


def solution(mesh):
    in_specs = (
        P(("seq", "head"), None),
        P(("seq", "head"), None),
        P(("seq", "head"), None),
        P("head", None),
        P("head"),
        P("seq", None),
        P(),
    )
    out_specs = P(("seq", "head"), None)
    return jax.shard_map(
        on_device, mesh=mesh, in_specs=in_specs, out_specs=out_specs, check_vma=False
    )
```

```python
import functools

import jax
import jax.numpy as jnp
from jax import lax
from jax.experimental import pallas as pl
from jax.experimental.pallas import tpu as pltpu
from jax.sharding import PartitionSpec as P

HD = 128
LOG2E = 1.4426950408889634


def attend(query, keys, values, biases, scale):
    scaled = query.astype(jnp.float32) * scale
    high = scaled.astype(jnp.bfloat16)
    low = (scaled - high.astype(jnp.float32)).astype(jnp.bfloat16)
    query = jnp.concatenate([high, low], axis=1)
    scores = [
        lax.dot_general(
            query, jnp.concatenate([k, k], axis=1), (((1,), (1,)), ((), ())),
            preferred_element_type=jnp.float32)
        for k in keys
    ]
    row_max = None
    for s, b in zip(scores, biases):
        top = jnp.max(s, axis=1, keepdims=True) + b
        row_max = top if row_max is None else jnp.maximum(row_max, top)
    weights = jnp.concatenate(
        [jnp.exp2(s - (row_max - b)).astype(jnp.bfloat16) for s, b in zip(scores, biases)], axis=1)
    both = jnp.dot(
        weights, jnp.concatenate([values, jnp.ones_like(values)], axis=1),
        preferred_element_type=jnp.float32)
    return both[:, :HD] / both[:, HD:]


def kernel(
    heads, levels, kv_local, group,
    level_hbm, anchor_hbm, partners_hbm, places_hbm, keys_ref, values_ref, queries_ref, out_ref,
    level_ref, anchor_ref, partners_ref, places_ref, small_sem,
    kv, qbuf, obuf, full, part, part_in, head_out, head_in, carry, carry_in, table,
    own_sem, full_sem, own_q_sem,
    x_send, x_recv, q_send, q_recv, o_send, o_recv, lv_send, lv_recv,
    core_send, core_recv, head_send, head_recv, carry_send, carry_recv,
    last_sem, last_send, last_recv,
):
    me = lax.axis_index("head")
    seat = lax.axis_index("seq")
    t = keys_ref.shape[0]
    block = heads * t
    wide = group * HD
    anchors = places_ref.shape[1]
    scale = HD ** -0.5 * LOG2E
    mesh_id = pl.DeviceIdType.MESH
    bf16 = jnp.bfloat16
    sources = (keys_ref, values_ref)
    mine = lax.rem(seat, 2)

    def peer(d):
        return lax.rem(me + d, heads)

    def partner(l):
        bit = lax.rem(lax.div(seat, 1 << l), 2)
        return seat + (1 - 2 * bit) * (1 << l)

    def cols(owner, j, width):
        return pl.ds(pl.multiple_of((owner * kv_local + j) * width, width), width)

    def rows(n, r):
        return pl.ds(pl.multiple_of(n * block + r * t, t), t)

    anchor_rows = pl.ds((levels + 1) * block, anchors)

    def to_head(src, dst, send, recv, d):
        return pltpu.make_async_remote_copy(
            src_ref=src, dst_ref=dst, send_sem=send, recv_sem=recv,
            device_id={"head": peer(d)}, device_id_type=mesh_id)

    def to_level(src, dst, send, recv, l):
        return pltpu.make_async_remote_copy(
            src_ref=src, dst_ref=dst, send_sem=send, recv_sem=recv,
            device_id={"seq": partner(l)}, device_id_type=mesh_id)

    def own_copy(j, c):
        return pltpu.make_async_copy(
            sources[c].at[:, cols(me, j, HD)], kv.at[j, c, rows(0, me)], own_sem.at[j, c])

    def full_copy(c):
        return pltpu.make_async_copy(sources[c], full.at[c], full_sem.at[c])

    def own_q(j):
        return pltpu.make_async_copy(
            queries_ref.at[:, cols(me, j, wide)], qbuf.at[j, 0], own_q_sem.at[j])

    def send_kv(j, c, d):
        return to_head(
            sources[c].at[:, cols(peer(d), j, HD)], kv.at[j, c, rows(0, me)],
            x_send.at[j, c, d], x_recv.at[j, c, d], d)

    def came_kv(j, c, d):
        return to_head(
            sources[c].at[:, cols(me, j, HD)], kv.at[j, c, rows(0, peer(heads - d))],
            x_send.at[j, c, d], x_recv.at[j, c, d], d)

    def send_q(j, d):
        return to_head(
            queries_ref.at[:, cols(peer(d), j, wide)], qbuf.at[j, d],
            q_send.at[j, d], q_recv.at[j, d], d)

    def send_level(j, c, d, l):
        r = peer(heads - d)
        src = sources[c].at[:, cols(me, j, HD)] if d == 0 else kv.at[j, c, rows(0, r)]
        return to_level(
            src, kv.at[j, c, rows(l + 1, r)],
            lv_send.at[j, c, d, l], lv_recv.at[j, c, d, l], l)

    def level_came(j, c, d, l):
        r = peer(heads - d)
        return to_level(
            kv.at[j, c, rows(0, r)], kv.at[j, c, rows(l + 1, r)],
            lv_send.at[j, c, d, l], lv_recv.at[j, c, d, l], l)

    def send_core():
        return to_level(part.at[1 - mine], part_in, core_send, core_recv, 0)

    def send_part(d):
        return to_head(head_out.at[d], head_in.at[d], head_send.at[d], head_recv.at[d], d)

    def send_carry(i, l):
        return to_level(carry.at[i], carry_in.at[i], carry_send.at[i], carry_recv.at[i], l)

    def own_last(j):
        return pltpu.make_async_copy(
            carry.at[levels - 1, j], kv.at[j, mine, anchor_rows], last_sem.at[j])

    def send_last(j):
        return to_level(
            carry.at[levels - 1, j], kv.at[j, mine, anchor_rows],
            last_send.at[j], last_recv.at[j], 0)

    def last_came(j):
        return to_level(
            carry.at[levels - 1, j], kv.at[j, 1 - mine, anchor_rows],
            last_send.at[j], last_recv.at[j], 0)

    def out_cols(owner, j, g):
        return pl.ds(pl.multiple_of(((owner * kv_local + j) * group + g) * HD, HD), HD)

    def send_out(j, g, d):
        return to_head(
            obuf.at[j, d, g], out_ref.at[:, out_cols(me, j, g)],
            o_send.at[j, g, d], o_recv.at[j, g, d], heads - d)

    def came_out(j, g, d):
        return to_head(
            obuf.at[j, d, g], out_ref.at[:, out_cols(peer(d), j, g)],
            o_send.at[j, g, d], o_recv.at[j, g, d], heads - d)

    def small(i):
        src = (level_hbm, anchor_hbm, partners_hbm, places_hbm)[i]
        dst = (level_ref, anchor_ref, partners_ref, places_ref)[i]
        return pltpu.make_async_copy(src, dst, small_sem.at[i])

    barrier = pltpu.get_barrier_semaphore()
    for d in range(1, heads):
        pl.semaphore_signal(barrier, inc=1, device_id={"head": peer(d)}, device_id_type=mesh_id)
    for l in range(levels):
        pl.semaphore_signal(barrier, inc=1, device_id={"seq": partner(l)}, device_id_type=mesh_id)

    for c in range(2):
        full_copy(c).start()
    for i in range(4):
        small(i).start()
    for j in range(kv_local):
        for c in range(2):
            own_copy(j, c).start()
        own_q(j).start()
    pl.semaphore_wait(barrier, heads - 1 + levels)

    far = list(reversed(range(levels)))

    def push_kv(j):
        for d in range(1, heads):
            for c in range(2):
                send_kv(j, c, d).start()

    def push_levels(j, c, d):
        for l in far:
            send_level(j, c, d, l).start()

    push_kv(0)
    for c in range(2):
        push_levels(0, c, 0)

    small(3).wait()
    first = (seat * heads + me) * t
    places = places_ref[...] - first
    token = lax.broadcasted_iota(jnp.int32, (t, anchors), 0)
    selector = jnp.where(places == token, 1.0, 0.0).astype(bf16)
    for c in range(2):
        full_copy(c).wait()
        for d in range(heads):
            for j in range(kv_local):
                part[c, d, j] = lax.dot_general(
                    selector, full[c, :, cols(peer(d), j, HD)], (((0,), (0,)), ((), ())),
                    preferred_element_type=jnp.float32).astype(bf16)
    send_core().start()
    send_core().wait_recv()
    for d in range(heads):
        head_out[d] = (
            part[mine, d].astype(jnp.float32) + part_in[d].astype(jnp.float32)).astype(bf16)
    for d in range(1, heads):
        send_part(d).start()
    for j in range(1, kv_local):
        push_kv(j)
    for j in range(kv_local):
        for d in range(1, heads):
            send_q(j, d).start()

    def wait_kv(j, c):
        own_copy(j, c).wait()
        for d in range(1, heads):
            came_kv(j, c, d).wait_recv()

    pending = [(0, c, d) for c in range(2) for d in range(1, heads)]
    for j in range(1, kv_local):
        pending += [(j, c, 0) for c in range(2)]
        pending += [(j, c, d) for c in range(2) for d in range(1, heads)]

    def push(count):
        for _ in range(min(count, len(pending))):
            j, c, d = pending.pop(0)
            if d == 0:
                own_copy(j, c).wait()
            else:
                came_kv(j, c, d).wait_recv()
            push_levels(j, c, d)

    for c in range(2):
        own_copy(0, c).wait()

    for i in range(3):
        small(i).wait()

    def fill(h, _):
        for l in range(levels):
            total = jnp.float32(0.0)
            for m in range(levels):
                total += jnp.where(partners_ref[0, m] == partner(l), level_ref[m, h], 0.0)
            table[l, h] = total * LOG2E
        table[levels, h] = anchor_ref[h] * LOG2E
        return 0

    lax.fori_loop(0, kv_local * group, fill, 0)

    held = head_out[0].astype(jnp.float32)
    for d in range(1, heads):
        send_part(d).wait_recv()
        held = held + head_in[d].astype(jnp.float32)
    carry[0] = held.astype(bf16)
    order = list(range(2, levels)) + ([1] if levels > 1 else [])
    for i, l in enumerate(order):
        send_carry(i, l).start()
        push(1)
        send_carry(i, l).wait_recv()
        carry[i + 1] = (
            carry[i].astype(jnp.float32) + carry_in[i].astype(jnp.float32)).astype(bf16)
    for j in range(kv_local):
        own_last(j).start()
        send_last(j).start()
    push(len(pending))

    def answer(j, d, g):
        return attend(
            qbuf[j, d, :, g * HD:(g + 1) * HD],
            [kv[j, 0, n * block:(n + 1) * block] for n in range(levels + 1)]
            + [kv[j, 0, (levels + 1) * block:]],
            kv[j, 1],
            [jnp.float32(0.0)] + [table[l, j * group + g] for l in range(levels + 1)],
            scale,
        ).astype(bf16)

    def one(j, _):
        own_last(j).wait()
        last_came(j).wait_recv()
        for l in range(levels):
            for c in range(2):
                for d in range(heads):
                    level_came(j, c, d, l).wait_recv()

        def remote(i, _):
            d = i + 1
            send_q(j, d).wait_recv()
            for g in range(group):
                obuf[j, d, g] = answer(j, d, g)
            for g in range(group):
                send_out(j, g, d).start()
            return 0

        lax.fori_loop(0, heads - 1, remote, 0)
        own_q(j).wait()
        for g in range(group):
            out_ref[:, out_cols(me, j, g)] = answer(j, 0, g)
        return 0

    lax.fori_loop(0, kv_local, one, 0)

    send_core().wait_send()
    for d in range(1, heads):
        send_part(d).wait_send()
    for i, l in enumerate(order):
        send_carry(i, l).wait_send()
    for j in range(kv_local):
        send_last(j).wait_send()
        for c in range(2):
            for d in range(heads):
                for l in range(levels):
                    send_level(j, c, d, l).wait_send()
            for d in range(1, heads):
                send_kv(j, c, d).wait_send()
        for d in range(1, heads):
            send_q(j, d).wait_send()
        for g in range(group):
            for d in range(1, heads):
                send_out(j, g, d).wait_send()
                came_out(j, g, d).wait_recv()


def on_device(queries, keys, values, level_bias, anchor_bias, partners, anchor_positions):
    t = queries.shape[0]
    heads = lax.axis_size("head")
    levels = lax.axis_size("seq").bit_length() - 1
    kv_local = keys.shape[1] // HD // heads
    group = level_bias.shape[0] // kv_local
    anchors = anchor_positions.shape[0]
    vmem = pl.BlockSpec(memory_space=pltpu.VMEM)
    hbm = pl.BlockSpec(memory_space=pl.ANY)
    dma = pltpu.SemaphoreType.DMA
    anchor_shape = (kv_local, anchors, HD)
    bf16 = jnp.bfloat16
    grant = (61 << 20) - 500_000 - queries.size * queries.dtype.itemsize
    return pl.pallas_call(
        functools.partial(kernel, heads, levels, kv_local, group),
        in_specs=[hbm] * 7,
        out_specs=vmem,
        out_shape=pltpu.VMEM(queries.shape, queries.dtype),
        scratch_shapes=[
            pltpu.SMEM(level_bias.shape[::-1], level_bias.dtype),
            pltpu.SMEM(anchor_bias.shape, anchor_bias.dtype),
            pltpu.SMEM(partners.shape, partners.dtype),
            pltpu.VMEM((1, anchors), anchor_positions.dtype),
            dma((4,)),
            pltpu.VMEM((kv_local, 2, (levels + 1) * heads * t + anchors, HD), bf16),
            pltpu.VMEM((kv_local, heads, t, group * HD), bf16),
            pltpu.VMEM((kv_local, heads, group, t, HD), bf16),
            pltpu.VMEM((2,) + keys.shape, bf16),
            pltpu.VMEM((2, heads) + anchor_shape, bf16),
            pltpu.VMEM((heads,) + anchor_shape, bf16),
            pltpu.VMEM((heads,) + anchor_shape, bf16),
            pltpu.VMEM((heads,) + anchor_shape, bf16),
            pltpu.VMEM((levels,) + anchor_shape, bf16),
            pltpu.VMEM((levels,) + anchor_shape, bf16),
            pltpu.SMEM((levels + 1, kv_local * group), jnp.float32),
            dma((kv_local, 2)), dma((2,)), dma((kv_local,)),
            dma((kv_local, 2, heads)), dma((kv_local, 2, heads)),
            dma((kv_local, heads)), dma((kv_local, heads)),
            dma((kv_local, group, heads)), dma((kv_local, group, heads)),
            dma((kv_local, 2, heads, levels)), dma((kv_local, 2, heads, levels)),
            dma, dma, dma((heads,)), dma((heads,)), dma((levels,)), dma((levels,)),
            dma((kv_local,)), dma((kv_local,)), dma((kv_local,)),
        ],
        compiler_params=pltpu.CompilerParams(
            vmem_limit_bytes=grant, collective_id=0, has_side_effects=True),
        name="attend",
    )(level_bias.T, anchor_bias, partners, anchor_positions[None, :], keys, values, queries)


def solution(mesh):
    in_specs = (
        P(("seq", "head"), None),
        P(("seq", "head"), None),
        P(("seq", "head"), None),
        P("head", None),
        P("head"),
        P("seq", None),
        P(),
    )
    out_specs = P(("seq", "head"), None)
    return jax.shard_map(
        on_device, mesh=mesh, in_specs=in_specs, out_specs=out_specs, check_vma=False
    )
```

```python
import functools

import jax
import jax.numpy as jnp
from jax import lax
from jax.experimental import pallas as pl
from jax.experimental.pallas import tpu as pltpu
from jax.sharding import PartitionSpec as P

HD = 128
LOG2E = 1.4426950408889634


def attend(query, keys, values, biases, scale):
    scaled = query.astype(jnp.float32) * scale
    high = scaled.astype(jnp.bfloat16)
    low = (scaled - high.astype(jnp.float32)).astype(jnp.bfloat16)
    query = jnp.concatenate([high, low], axis=1)
    scores = [
        lax.dot_general(
            query, jnp.concatenate([k, k], axis=1), (((1,), (1,)), ((), ())),
            preferred_element_type=jnp.float32)
        for k in keys
    ]
    row_max = None
    for s, b in zip(scores, biases):
        top = jnp.max(s, axis=1, keepdims=True) + b
        row_max = top if row_max is None else jnp.maximum(row_max, top)
    weights = jnp.concatenate(
        [jnp.exp2(s - (row_max - b)).astype(jnp.bfloat16) for s, b in zip(scores, biases)], axis=1)
    both = jnp.dot(
        weights, jnp.concatenate([values, jnp.ones_like(values)], axis=1),
        preferred_element_type=jnp.float32)
    return both[:, :HD] / both[:, HD:]


def kernel(
    heads, levels, kv_local, group,
    level_hbm, anchor_hbm, partners_hbm, places_hbm, keys_ref, values_ref, queries_ref, out_ref,
    level_ref, anchor_ref, partners_ref, places_ref, small_sem,
    kv, qbuf, obuf, full, part, part_in, head_out, head_in, pair, pair_in, carry, carry_in, table,
    own_sem, full_sem, own_q_sem,
    x_send, x_recv, q_send, q_recv, o_send, o_recv, lv_send, lv_recv,
    core_send, core_recv, head_send, head_recv, pair_send, pair_recv, carry_send, carry_recv,
    last_sem, half_send, half_recv, last_send, last_recv,
):
    me = lax.axis_index("head")
    seat = lax.axis_index("seq")
    t = keys_ref.shape[0]
    block = heads * t
    wide = group * HD
    anchors = places_ref.shape[1]
    scale = HD ** -0.5 * LOG2E
    mesh_id = pl.DeviceIdType.MESH
    bf16 = jnp.bfloat16
    sources = (keys_ref, values_ref)
    mine = lax.rem(seat, 2)
    side = lax.rem(lax.div(seat, 2), 2)
    half = anchors // 2

    def peer(d):
        return lax.rem(me + d, heads)

    def partner(l):
        bit = lax.rem(lax.div(seat, 1 << l), 2)
        return seat + (1 - 2 * bit) * (1 << l)

    def cols(owner, j, width):
        return pl.ds(pl.multiple_of((owner * kv_local + j) * width, width), width)

    def rows(n, r):
        return pl.ds(pl.multiple_of(n * block + r * t, t), t)

    anchor_rows = pl.ds((levels + 1) * block, anchors)

    def half_rows(which):
        return pl.ds(pl.multiple_of((levels + 1) * block + which * half, 16), half)

    def to_head(src, dst, send, recv, d):
        return pltpu.make_async_remote_copy(
            src_ref=src, dst_ref=dst, send_sem=send, recv_sem=recv,
            device_id={"head": peer(d)}, device_id_type=mesh_id)

    def to_level(src, dst, send, recv, l):
        return pltpu.make_async_remote_copy(
            src_ref=src, dst_ref=dst, send_sem=send, recv_sem=recv,
            device_id={"seq": partner(l)}, device_id_type=mesh_id)

    def own_copy(j, c):
        return pltpu.make_async_copy(
            sources[c].at[:, cols(me, j, HD)], kv.at[j, c, rows(0, me)], own_sem.at[j, c])

    def full_copy(c):
        return pltpu.make_async_copy(sources[c], full.at[c], full_sem.at[c])

    def own_q(j):
        return pltpu.make_async_copy(
            queries_ref.at[:, cols(me, j, wide)], qbuf.at[j, 0], own_q_sem.at[j])

    def send_kv(j, c, d):
        return to_head(
            sources[c].at[:, cols(peer(d), j, HD)], kv.at[j, c, rows(0, me)],
            x_send.at[j, c, d], x_recv.at[j, c, d], d)

    def came_kv(j, c, d):
        return to_head(
            sources[c].at[:, cols(me, j, HD)], kv.at[j, c, rows(0, peer(heads - d))],
            x_send.at[j, c, d], x_recv.at[j, c, d], d)

    def send_q(j, d):
        return to_head(
            queries_ref.at[:, cols(peer(d), j, wide)], qbuf.at[j, d],
            q_send.at[j, d], q_recv.at[j, d], d)

    def send_level(j, c, d, l):
        r = peer(heads - d)
        src = sources[c].at[:, cols(me, j, HD)] if d == 0 else kv.at[j, c, rows(0, r)]
        return to_level(
            src, kv.at[j, c, rows(l + 1, r)],
            lv_send.at[j, c, d, l], lv_recv.at[j, c, d, l], l)

    def level_came(j, c, d, l):
        r = peer(heads - d)
        return to_level(
            kv.at[j, c, rows(0, r)], kv.at[j, c, rows(l + 1, r)],
            lv_send.at[j, c, d, l], lv_recv.at[j, c, d, l], l)

    def send_core():
        return to_level(part.at[1 - mine], part_in, core_send, core_recv, 0)

    def send_part(d):
        return to_head(head_out.at[peer(d)], head_in.at[d], head_send.at[d], head_recv.at[d], d)

    def send_pair():
        return to_level(pair.at[1 - side], pair_in, pair_send, pair_recv, 1)

    def send_carry(i, l):
        return to_level(carry.at[i], carry_in.at[i], carry_send.at[i], carry_recv.at[i], l)

    def own_half(j):
        return pltpu.make_async_copy(
            carry.at[levels - 2, j], kv.at[j, mine, half_rows(side)], last_sem.at[j])

    def send_half(j):
        return to_level(
            carry.at[levels - 2, j], kv.at[j, mine, half_rows(side)],
            half_send.at[j], half_recv.at[j], 1)

    def half_came(j):
        return to_level(
            carry.at[levels - 2, j], kv.at[j, mine, half_rows(1 - side)],
            half_send.at[j], half_recv.at[j], 1)

    def send_last(j):
        return to_level(
            kv.at[j, mine, anchor_rows], kv.at[j, mine, anchor_rows],
            last_send.at[j], last_recv.at[j], 0)

    def last_came(j):
        return to_level(
            kv.at[j, mine, anchor_rows], kv.at[j, 1 - mine, anchor_rows],
            last_send.at[j], last_recv.at[j], 0)

    def out_cols(owner, j, g):
        return pl.ds(pl.multiple_of(((owner * kv_local + j) * group + g) * HD, HD), HD)

    def send_out(j, g, d):
        return to_head(
            obuf.at[j, d, g], out_ref.at[:, out_cols(me, j, g)],
            o_send.at[j, g, d], o_recv.at[j, g, d], heads - d)

    def came_out(j, g, d):
        return to_head(
            obuf.at[j, d, g], out_ref.at[:, out_cols(peer(d), j, g)],
            o_send.at[j, g, d], o_recv.at[j, g, d], heads - d)

    def small(i):
        src = (level_hbm, anchor_hbm, partners_hbm, places_hbm)[i]
        dst = (level_ref, anchor_ref, partners_ref, places_ref)[i]
        return pltpu.make_async_copy(src, dst, small_sem.at[i])

    barrier = pltpu.get_barrier_semaphore()
    for d in range(1, heads):
        pl.semaphore_signal(barrier, inc=1, device_id={"head": peer(d)}, device_id_type=mesh_id)
    for l in range(levels):
        pl.semaphore_signal(barrier, inc=1, device_id={"seq": partner(l)}, device_id_type=mesh_id)

    for c in range(2):
        full_copy(c).start()
    for i in range(4):
        small(i).start()
    for j in range(kv_local):
        for c in range(2):
            own_copy(j, c).start()
        own_q(j).start()
    pl.semaphore_wait(barrier, heads - 1 + levels)

    far = list(reversed(range(levels)))

    def push_kv(j):
        for d in range(1, heads):
            for c in range(2):
                send_kv(j, c, d).start()

    def push_levels(j, c, d):
        for l in far:
            send_level(j, c, d, l).start()

    push_kv(0)
    for c in range(2):
        push_levels(0, c, 0)

    small(3).wait()
    first = (seat * heads + me) * t
    places = places_ref[...] - first
    token = lax.broadcasted_iota(jnp.int32, (t, anchors), 0)
    selector = jnp.where(places == token, 1.0, 0.0).astype(bf16)
    for c in range(2):
        full_copy(c).wait()
        found = lax.dot_general(
            selector, full[c], (((0,), (0,)), ((), ())), preferred_element_type=jnp.float32)
        found = found.astype(bf16)
        for owner in range(heads):
            for j in range(kv_local):
                at = (owner * kv_local + j) * HD
                part[c, owner, j] = found[:, at:at + HD]
    send_core().start()
    send_core().wait_recv()
    for d in range(heads):
        head_out[d] = (
            part[mine, d].astype(jnp.float32) + part_in[d].astype(jnp.float32)).astype(bf16)
    for d in range(1, heads):
        send_part(d).start()
    for j in range(1, kv_local):
        push_kv(j)
    for j in range(kv_local):
        for d in range(1, heads):
            send_q(j, d).start()

    def wait_kv(j, c):
        own_copy(j, c).wait()
        for d in range(1, heads):
            came_kv(j, c, d).wait_recv()

    pending = [(0, c, d) for c in range(2) for d in range(1, heads)]
    for j in range(1, kv_local):
        pending += [(j, c, 0) for c in range(2)]
        pending += [(j, c, d) for c in range(2) for d in range(1, heads)]

    def push(count):
        for _ in range(min(count, len(pending))):
            j, c, d = pending.pop(0)
            if d == 0:
                own_copy(j, c).wait()
            else:
                came_kv(j, c, d).wait_recv()
            push_levels(j, c, d)

    for c in range(2):
        own_copy(0, c).wait()

    def fill_table():
        for i in range(3):
            small(i).wait()
        match = [[jnp.where(partners_ref[0, m] == partner(l), LOG2E, 0.0) for m in range(levels)]
                 for l in range(levels)]

        def fill(h, _):
            biases = [level_ref[m, h] for m in range(levels)]
            for l in range(levels):
                table[l, h] = sum(match[l][m] * biases[m] for m in range(levels))
            table[levels, h] = anchor_ref[h] * LOG2E
            return 0

        lax.fori_loop(0, kv_local * group, fill, 0)

    held = head_out[me].astype(jnp.float32)
    for d in range(1, heads):
        send_part(d).wait_recv()
        held = held + head_in[d].astype(jnp.float32)
    for which in range(2):
        pair[which] = held[:, which * half:(which + 1) * half].astype(bf16)
    send_pair().start()
    push(1)
    fill_table()
    send_pair().wait_recv()
    carry[0] = (pair[side].astype(jnp.float32) + pair_in[...].astype(jnp.float32)).astype(bf16)
    order = list(range(2, levels))
    for i, l in enumerate(order):
        send_carry(i, l).start()
        push(2 if i else 1)
        send_carry(i, l).wait_recv()
        carry[i + 1] = (
            carry[i].astype(jnp.float32) + carry_in[i].astype(jnp.float32)).astype(bf16)
    for j in range(kv_local):
        own_half(j).start()
        send_half(j).start()
    push(2)
    for j in range(kv_local):
        own_half(j).wait()
        half_came(j).wait_recv()
        send_last(j).start()
    push(len(pending))

    def answer(j, d, g):
        return attend(
            qbuf[j, d, :, g * HD:(g + 1) * HD],
            [kv[j, 0, n * block:(n + 1) * block] for n in range(levels + 1)]
            + [kv[j, 0, (levels + 1) * block:]],
            kv[j, 1],
            [jnp.float32(0.0)] + [table[l, j * group + g] for l in range(levels + 1)],
            scale,
        ).astype(bf16)

    def one(j, _):
        last_came(j).wait_recv()
        for l in range(levels):
            for c in range(2):
                for d in range(heads):
                    level_came(j, c, d, l).wait_recv()

        def remote(i, _):
            d = i + 1
            send_q(j, d).wait_recv()
            for g in range(group):
                obuf[j, d, g] = answer(j, d, g)
            for g in range(group):
                send_out(j, g, d).start()
            return 0

        lax.fori_loop(0, heads - 1, remote, 0)
        own_q(j).wait()
        for g in range(group):
            out_ref[:, out_cols(me, j, g)] = answer(j, 0, g)
        return 0

    lax.fori_loop(0, kv_local, one, 0)

    send_core().wait_send()
    send_pair().wait_send()
    for d in range(1, heads):
        send_part(d).wait_send()
    for i, l in enumerate(order):
        send_carry(i, l).wait_send()
    for j in range(kv_local):
        send_half(j).wait_send()
        send_last(j).wait_send()
        for c in range(2):
            for d in range(heads):
                for l in range(levels):
                    send_level(j, c, d, l).wait_send()
            for d in range(1, heads):
                send_kv(j, c, d).wait_send()
        for d in range(1, heads):
            send_q(j, d).wait_send()
        for g in range(group):
            for d in range(1, heads):
                send_out(j, g, d).wait_send()
                came_out(j, g, d).wait_recv()


def on_device(queries, keys, values, level_bias, anchor_bias, partners, anchor_positions):
    t = queries.shape[0]
    heads = lax.axis_size("head")
    levels = lax.axis_size("seq").bit_length() - 1
    kv_local = keys.shape[1] // HD // heads
    group = level_bias.shape[0] // kv_local
    anchors = anchor_positions.shape[0]
    vmem = pl.BlockSpec(memory_space=pltpu.VMEM)
    hbm = pl.BlockSpec(memory_space=pl.ANY)
    dma = pltpu.SemaphoreType.DMA
    anchor_shape = (kv_local, anchors, HD)
    half_shape = (kv_local, anchors // 2, HD)
    bf16 = jnp.bfloat16
    grant = (61 << 20) - 500_000 - queries.size * queries.dtype.itemsize
    return pl.pallas_call(
        functools.partial(kernel, heads, levels, kv_local, group),
        in_specs=[hbm] * 7,
        out_specs=vmem,
        out_shape=pltpu.VMEM(queries.shape, queries.dtype),
        scratch_shapes=[
            pltpu.SMEM(level_bias.shape[::-1], level_bias.dtype),
            pltpu.SMEM(anchor_bias.shape, anchor_bias.dtype),
            pltpu.SMEM(partners.shape, partners.dtype),
            pltpu.VMEM((1, anchors), anchor_positions.dtype),
            dma((4,)),
            pltpu.VMEM((kv_local, 2, (levels + 1) * heads * t + anchors, HD), bf16),
            pltpu.VMEM((kv_local, heads, t, group * HD), bf16),
            pltpu.VMEM((kv_local, heads, group, t, HD), bf16),
            pltpu.VMEM((2,) + keys.shape, bf16),
            pltpu.VMEM((2, heads) + anchor_shape, bf16),
            pltpu.VMEM((heads,) + anchor_shape, bf16),
            pltpu.VMEM((heads,) + anchor_shape, bf16),
            pltpu.VMEM((heads,) + anchor_shape, bf16),
            pltpu.VMEM((2,) + half_shape, bf16),
            pltpu.VMEM(half_shape, bf16),
            pltpu.VMEM((levels,) + half_shape, bf16),
            pltpu.VMEM((levels,) + half_shape, bf16),
            pltpu.SMEM((levels + 1, kv_local * group), jnp.float32),
            dma((kv_local, 2)), dma((2,)), dma((kv_local,)),
            dma((kv_local, 2, heads)), dma((kv_local, 2, heads)),
            dma((kv_local, heads)), dma((kv_local, heads)),
            dma((kv_local, group, heads)), dma((kv_local, group, heads)),
            dma((kv_local, 2, heads, levels)), dma((kv_local, 2, heads, levels)),
            dma, dma, dma((heads,)), dma((heads,)), dma, dma, dma((levels,)), dma((levels,)),
            dma((kv_local,)), dma((kv_local,)), dma((kv_local,)), dma((kv_local,)), dma((kv_local,)),
        ],
        compiler_params=pltpu.CompilerParams(
            vmem_limit_bytes=grant, collective_id=0, has_side_effects=True),
        name="attend",
    )(level_bias.T, anchor_bias, partners, anchor_positions[None, :], keys, values, queries)


def solution(mesh):
    in_specs = (
        P(("seq", "head"), None),
        P(("seq", "head"), None),
        P(("seq", "head"), None),
        P("head", None),
        P("head"),
        P("seq", None),
        P(),
    )
    out_specs = P(("seq", "head"), None)
    return jax.shard_map(
        on_device, mesh=mesh, in_specs=in_specs, out_specs=out_specs, check_vma=False
    )
```

```python
import functools

import jax
import jax.numpy as jnp
from jax import lax
from jax.experimental import pallas as pl
from jax.experimental.pallas import tpu as pltpu
from jax.sharding import PartitionSpec as P

HD = 128
LOG2E = 1.4426950408889634


def attend(query, keys, values, biases, scale):
    scaled = query.astype(jnp.float32) * scale
    high = scaled.astype(jnp.bfloat16)
    low = (scaled - high.astype(jnp.float32)).astype(jnp.bfloat16)
    query = jnp.concatenate([high, low], axis=1)
    scores = [
        lax.dot_general(
            query, jnp.concatenate([k, k], axis=1), (((1,), (1,)), ((), ())),
            preferred_element_type=jnp.float32)
        for k in keys
    ]
    row_max = None
    for s, b in zip(scores, biases):
        top = jnp.max(s, axis=1, keepdims=True) + b
        row_max = top if row_max is None else jnp.maximum(row_max, top)
    weights = jnp.concatenate(
        [jnp.exp2(s - (row_max - b)).astype(jnp.bfloat16) for s, b in zip(scores, biases)], axis=1)
    both = jnp.dot(
        weights, jnp.concatenate([values, jnp.ones_like(values)], axis=1),
        preferred_element_type=jnp.float32)
    return both[:, :HD] / both[:, HD:]


def kernel(
    heads, levels, kv_local, group,
    level_hbm, anchor_hbm, partners_hbm, places_hbm, keys_ref, values_ref, queries_ref, out_ref,
    level_ref, anchor_ref, partners_ref, places_ref, small_sem,
    kv, qbuf, obuf, full, part, part_in, head_out, head_in, pair, pair_in, carry, carry_in, table,
    own_sem, full_sem, own_q_sem,
    x_send, x_recv, q_send, q_recv, o_send, o_recv, lv_send, lv_recv,
    core_send, core_recv, head_send, head_recv, pair_send, pair_recv, carry_send, carry_recv,
    last_sem, half_send, half_recv, last_send, last_recv,
):
    me = lax.axis_index("head")
    seat = lax.axis_index("seq")
    t = keys_ref.shape[0]
    block = heads * t
    wide = group * HD
    anchors = places_ref.shape[1]
    scale = HD ** -0.5 * LOG2E
    mesh_id = pl.DeviceIdType.MESH
    bf16 = jnp.bfloat16
    sources = (keys_ref, values_ref)
    mine = lax.rem(seat, 2)
    side = lax.rem(lax.div(seat, 2), 2)
    half = anchors // 2

    def peer(d):
        return lax.rem(me + d, heads)

    def partner(l):
        bit = lax.rem(lax.div(seat, 1 << l), 2)
        return seat + (1 - 2 * bit) * (1 << l)

    def cols(owner, j, width):
        return pl.ds(pl.multiple_of((owner * kv_local + j) * width, width), width)

    def rows(n, r):
        return pl.ds(pl.multiple_of(n * block + r * t, t), t)

    anchor_rows = pl.ds((levels + 1) * block, anchors)

    def half_rows(which):
        return pl.ds(pl.multiple_of((levels + 1) * block + which * half, 16), half)

    def to_head(src, dst, send, recv, d):
        return pltpu.make_async_remote_copy(
            src_ref=src, dst_ref=dst, send_sem=send, recv_sem=recv,
            device_id={"head": peer(d)}, device_id_type=mesh_id)

    def to_level(src, dst, send, recv, l):
        return pltpu.make_async_remote_copy(
            src_ref=src, dst_ref=dst, send_sem=send, recv_sem=recv,
            device_id={"seq": partner(l)}, device_id_type=mesh_id)

    def own_copy(j, c):
        return pltpu.make_async_copy(
            sources[c].at[:, cols(me, j, HD)], kv.at[j, c, rows(0, me)], own_sem.at[j, c])

    def full_copy(c):
        return pltpu.make_async_copy(sources[c], full.at[c], full_sem.at[c])

    def own_q(j):
        return pltpu.make_async_copy(
            queries_ref.at[:, cols(me, j, wide)], qbuf.at[j, 0], own_q_sem.at[j])

    def send_kv(j, c, d):
        return to_head(
            sources[c].at[:, cols(peer(d), j, HD)], kv.at[j, c, rows(0, me)],
            x_send.at[j, c, d], x_recv.at[j, c, d], d)

    def came_kv(j, c, d):
        return to_head(
            sources[c].at[:, cols(me, j, HD)], kv.at[j, c, rows(0, peer(heads - d))],
            x_send.at[j, c, d], x_recv.at[j, c, d], d)

    def send_q(j, d):
        return to_head(
            queries_ref.at[:, cols(peer(d), j, wide)], qbuf.at[j, d],
            q_send.at[j, d], q_recv.at[j, d], d)

    def send_level(j, c, d, l):
        r = peer(heads - d)
        src = sources[c].at[:, cols(me, j, HD)] if d == 0 else kv.at[j, c, rows(0, r)]
        return to_level(
            src, kv.at[j, c, rows(l + 1, r)],
            lv_send.at[j, c, d, l], lv_recv.at[j, c, d, l], l)

    def level_came(j, c, d, l):
        r = peer(heads - d)
        return to_level(
            kv.at[j, c, rows(0, r)], kv.at[j, c, rows(l + 1, r)],
            lv_send.at[j, c, d, l], lv_recv.at[j, c, d, l], l)

    def send_core():
        return to_level(part.at[1 - mine], part_in, core_send, core_recv, 0)

    def send_part(d):
        return to_head(head_out.at[peer(d)], head_in.at[d], head_send.at[d], head_recv.at[d], d)

    def send_pair():
        return to_level(pair.at[1 - side], pair_in, pair_send, pair_recv, 1)

    def send_carry(i, l):
        return to_level(carry.at[i], carry_in.at[i], carry_send.at[i], carry_recv.at[i], l)

    def own_half(j):
        return pltpu.make_async_copy(
            carry.at[levels - 2, j], kv.at[j, mine, half_rows(side)], last_sem.at[j])

    def send_half(j):
        return to_level(
            carry.at[levels - 2, j], kv.at[j, mine, half_rows(side)],
            half_send.at[j], half_recv.at[j], 1)

    def half_came(j):
        return to_level(
            carry.at[levels - 2, j], kv.at[j, mine, half_rows(1 - side)],
            half_send.at[j], half_recv.at[j], 1)

    def send_last(j):
        return to_level(
            kv.at[j, mine, anchor_rows], kv.at[j, mine, anchor_rows],
            last_send.at[j], last_recv.at[j], 0)

    def last_came(j):
        return to_level(
            kv.at[j, mine, anchor_rows], kv.at[j, 1 - mine, anchor_rows],
            last_send.at[j], last_recv.at[j], 0)

    def out_cols(owner, j, g):
        return pl.ds(pl.multiple_of(((owner * kv_local + j) * group + g) * HD, HD), HD)

    def send_out(j, g, d):
        return to_head(
            obuf.at[j, d, g], out_ref.at[:, out_cols(me, j, g)],
            o_send.at[j, g, d], o_recv.at[j, g, d], heads - d)

    def came_out(j, g, d):
        return to_head(
            obuf.at[j, d, g], out_ref.at[:, out_cols(peer(d), j, g)],
            o_send.at[j, g, d], o_recv.at[j, g, d], heads - d)

    def small(i):
        src = (level_hbm, anchor_hbm, partners_hbm, places_hbm)[i]
        dst = (level_ref, anchor_ref, partners_ref, places_ref)[i]
        return pltpu.make_async_copy(src, dst, small_sem.at[i])

    barrier = pltpu.get_barrier_semaphore()
    for d in range(1, heads):
        pl.semaphore_signal(barrier, inc=1, device_id={"head": peer(d)}, device_id_type=mesh_id)
    for l in range(levels):
        pl.semaphore_signal(barrier, inc=1, device_id={"seq": partner(l)}, device_id_type=mesh_id)

    for c in range(2):
        full_copy(c).start()
    for i in range(4):
        small(i).start()
    for j in range(kv_local):
        for c in range(2):
            own_copy(j, c).start()
        own_q(j).start()
    pl.semaphore_wait(barrier, heads - 1 + levels)

    far = list(reversed(range(levels)))

    def push_kv(j):
        for d in range(1, heads):
            for c in range(2):
                send_kv(j, c, d).start()

    def push_levels(j, c, d):
        for l in far:
            send_level(j, c, d, l).start()

    push_kv(0)
    for c in range(2):
        push_levels(0, c, 0)

    small(3).wait()
    first = (seat * heads + me) * t
    places = places_ref[...] - first
    token = lax.broadcasted_iota(jnp.int32, (t, anchors), 0)
    selector = jnp.where(places == token, 1.0, 0.0).astype(bf16)
    for c in range(2):
        full_copy(c).wait()
        found = lax.dot_general(
            selector, full[c], (((0,), (0,)), ((), ())), preferred_element_type=jnp.float32)
        found = found.astype(bf16)
        for owner in range(heads):
            for j in range(kv_local):
                at = (owner * kv_local + j) * HD
                part[c, owner, j] = found[:, at:at + HD]
    send_core().start()
    send_core().wait_recv()
    for d in range(heads):
        head_out[d] = (
            part[mine, d].astype(jnp.float32) + part_in[d].astype(jnp.float32)).astype(bf16)
    for d in range(1, heads):
        send_part(d).start()
    for j in range(1, kv_local):
        push_kv(j)
    for j in range(kv_local):
        for d in range(1, heads):
            send_q(j, d).start()

    def wait_kv(j, c):
        own_copy(j, c).wait()
        for d in range(1, heads):
            came_kv(j, c, d).wait_recv()

    pending = [(0, c, d) for c in range(2) for d in range(1, heads)]
    for j in range(1, kv_local):
        pending += [(j, c, 0) for c in range(2)]
        pending += [(j, c, d) for c in range(2) for d in range(1, heads)]

    def push(count):
        for _ in range(min(count, len(pending))):
            j, c, d = pending.pop(0)
            if d == 0:
                own_copy(j, c).wait()
            else:
                came_kv(j, c, d).wait_recv()
            push_levels(j, c, d)

    for c in range(2):
        own_copy(0, c).wait()

    def fill_table():
        for i in range(3):
            small(i).wait()
        match = [[jnp.where(partners_ref[0, m] == partner(l), LOG2E, 0.0) for m in range(levels)]
                 for l in range(levels)]

        def fill(h, _):
            biases = [level_ref[m, h] for m in range(levels)]
            for l in range(levels):
                table[l, h] = sum(match[l][m] * biases[m] for m in range(levels))
            table[levels, h] = anchor_ref[h] * LOG2E
            return 0

        lax.fori_loop(0, kv_local * group, fill, 0)

    held = head_out[me].astype(jnp.float32)
    for d in range(1, heads):
        send_part(d).wait_recv()
        held = held + head_in[d].astype(jnp.float32)
    for which in range(2):
        pair[which] = held[:, which * half:(which + 1) * half].astype(bf16)
    send_pair().start()
    push(1)
    fill_table()
    send_pair().wait_recv()
    carry[0] = (pair[side].astype(jnp.float32) + pair_in[...].astype(jnp.float32)).astype(bf16)
    order = list(range(2, levels))
    for i, l in enumerate(order):
        send_carry(i, l).start()
        push(1)
        send_carry(i, l).wait_recv()
        carry[i + 1] = (
            carry[i].astype(jnp.float32) + carry_in[i].astype(jnp.float32)).astype(bf16)
    for j in range(kv_local):
        own_half(j).start()
        send_half(j).start()
    push(2)
    for j in range(kv_local):
        own_half(j).wait()
        half_came(j).wait_recv()
        send_last(j).start()
    push(len(pending))

    def answer(j, d, g):
        return attend(
            qbuf[j, d, :, g * HD:(g + 1) * HD],
            [kv[j, 0, n * block:(n + 1) * block] for n in range(levels + 1)]
            + [kv[j, 0, (levels + 1) * block:]],
            kv[j, 1],
            [jnp.float32(0.0)] + [table[l, j * group + g] for l in range(levels + 1)],
            scale,
        ).astype(bf16)

    def one(j, _):
        last_came(j).wait_recv()
        for l in range(levels):
            for c in range(2):
                for d in range(heads):
                    level_came(j, c, d, l).wait_recv()

        def remote(i, _):
            d = i + 1
            send_q(j, d).wait_recv()
            for g in range(group):
                obuf[j, d, g] = answer(j, d, g)
            for g in range(group):
                send_out(j, g, d).start()
            return 0

        lax.fori_loop(0, heads - 1, remote, 0)
        own_q(j).wait()
        for g in range(group):
            out_ref[:, out_cols(me, j, g)] = answer(j, 0, g)
        return 0

    lax.fori_loop(0, kv_local, one, 0)

    send_core().wait_send()
    send_pair().wait_send()
    for d in range(1, heads):
        send_part(d).wait_send()
    for i, l in enumerate(order):
        send_carry(i, l).wait_send()
    for j in range(kv_local):
        send_half(j).wait_send()
        send_last(j).wait_send()
        for c in range(2):
            for d in range(heads):
                for l in range(levels):
                    send_level(j, c, d, l).wait_send()
            for d in range(1, heads):
                send_kv(j, c, d).wait_send()
        for d in range(1, heads):
            send_q(j, d).wait_send()
        for g in range(group):
            for d in range(1, heads):
                send_out(j, g, d).wait_send()
                came_out(j, g, d).wait_recv()


def on_device(queries, keys, values, level_bias, anchor_bias, partners, anchor_positions):
    t = queries.shape[0]
    heads = lax.axis_size("head")
    levels = lax.axis_size("seq").bit_length() - 1
    kv_local = keys.shape[1] // HD // heads
    group = level_bias.shape[0] // kv_local
    anchors = anchor_positions.shape[0]
    vmem = pl.BlockSpec(memory_space=pltpu.VMEM)
    hbm = pl.BlockSpec(memory_space=pl.ANY)
    dma = pltpu.SemaphoreType.DMA
    anchor_shape = (kv_local, anchors, HD)
    half_shape = (kv_local, anchors // 2, HD)
    bf16 = jnp.bfloat16
    grant = (61 << 20) - 500_000 - queries.size * queries.dtype.itemsize
    return pl.pallas_call(
        functools.partial(kernel, heads, levels, kv_local, group),
        in_specs=[hbm] * 7,
        out_specs=vmem,
        out_shape=pltpu.VMEM(queries.shape, queries.dtype),
        scratch_shapes=[
            pltpu.SMEM(level_bias.shape[::-1], level_bias.dtype),
            pltpu.SMEM(anchor_bias.shape, anchor_bias.dtype),
            pltpu.SMEM(partners.shape, partners.dtype),
            pltpu.VMEM((1, anchors), anchor_positions.dtype),
            dma((4,)),
            pltpu.VMEM((kv_local, 2, (levels + 1) * heads * t + anchors, HD), bf16),
            pltpu.VMEM((kv_local, heads, t, group * HD), bf16),
            pltpu.VMEM((kv_local, heads, group, t, HD), bf16),
            pltpu.VMEM((2,) + keys.shape, bf16),
            pltpu.VMEM((2, heads) + anchor_shape, bf16),
            pltpu.VMEM((heads,) + anchor_shape, bf16),
            pltpu.VMEM((heads,) + anchor_shape, bf16),
            pltpu.VMEM((heads,) + anchor_shape, bf16),
            pltpu.VMEM((2,) + half_shape, bf16),
            pltpu.VMEM(half_shape, bf16),
            pltpu.VMEM((levels,) + half_shape, bf16),
            pltpu.VMEM((levels,) + half_shape, bf16),
            pltpu.SMEM((levels + 1, kv_local * group), jnp.float32),
            dma((kv_local, 2)), dma((2,)), dma((kv_local,)),
            dma((kv_local, 2, heads)), dma((kv_local, 2, heads)),
            dma((kv_local, heads)), dma((kv_local, heads)),
            dma((kv_local, group, heads)), dma((kv_local, group, heads)),
            dma((kv_local, 2, heads, levels)), dma((kv_local, 2, heads, levels)),
            dma, dma, dma((heads,)), dma((heads,)), dma, dma, dma((levels,)), dma((levels,)),
            dma((kv_local,)), dma((kv_local,)), dma((kv_local,)), dma((kv_local,)), dma((kv_local,)),
        ],
        compiler_params=pltpu.CompilerParams(
            vmem_limit_bytes=grant, collective_id=0, has_side_effects=True),
        name="attend",
    )(level_bias.T, anchor_bias, partners, anchor_positions[None, :], keys, values, queries)


def solution(mesh):
    in_specs = (
        P(("seq", "head"), None),
        P(("seq", "head"), None),
        P(("seq", "head"), None),
        P("head", None),
        P("head"),
        P("seq", None),
        P(),
    )
    out_specs = P(("seq", "head"), None)
    return jax.shard_map(
        on_device, mesh=mesh, in_specs=in_specs, out_specs=out_specs, check_vma=False
    )
```

```python
import functools

import jax
import jax.numpy as jnp
from jax import lax
from jax.experimental import pallas as pl
from jax.experimental.pallas import tpu as pltpu
from jax.sharding import PartitionSpec as P

HD = 128
LOG2E = 1.4426950408889634


def attend(query, keys, values, biases, scale):
    scaled = query.astype(jnp.float32) * scale
    high = scaled.astype(jnp.bfloat16)
    low = (scaled - high.astype(jnp.float32)).astype(jnp.bfloat16)
    query = jnp.concatenate([high, low], axis=1)
    scores = [
        lax.dot_general(
            query, jnp.concatenate([k, k], axis=1), (((1,), (1,)), ((), ())),
            preferred_element_type=jnp.float32)
        for k in keys
    ]
    row_max = None
    for s, b in zip(scores, biases):
        top = jnp.max(s, axis=1, keepdims=True) + b
        row_max = top if row_max is None else jnp.maximum(row_max, top)
    weights = jnp.concatenate(
        [jnp.exp2(s - (row_max - b)).astype(jnp.bfloat16) for s, b in zip(scores, biases)], axis=1)
    both = jnp.dot(
        weights, jnp.concatenate([values, jnp.ones_like(values)], axis=1),
        preferred_element_type=jnp.float32)
    return both[:, :HD] / both[:, HD:]


def kernel(
    heads, levels, kv_local, group,
    level_hbm, anchor_hbm, partners_hbm, places_hbm, keys_ref, values_ref, queries_ref, out_ref,
    level_ref, anchor_ref, partners_ref, places_ref, small_sem,
    kv, qbuf, obuf, full, part, part_in, head_out, head_in, pair, pair_in, carry, carry_in, table,
    own_sem, full_sem, own_q_sem,
    x_send, x_recv, q_send, q_recv, o_send, o_recv, lv_send, lv_recv,
    core_send, core_recv, head_send, head_recv, pair_send, pair_recv, carry_send, carry_recv,
    last_sem, half_send, half_recv, last_send, last_recv,
):
    me = lax.axis_index("head")
    seat = lax.axis_index("seq")
    t = keys_ref.shape[0]
    block = heads * t
    wide = group * HD
    anchors = places_ref.shape[1]
    scale = HD ** -0.5 * LOG2E
    mesh_id = pl.DeviceIdType.MESH
    bf16 = jnp.bfloat16
    sources = (keys_ref, values_ref)
    mine = lax.rem(seat, 2)
    side = lax.rem(lax.div(seat, 2), 2)
    half = anchors // 2

    def peer(d):
        return lax.rem(me + d, heads)

    def partner(l):
        bit = lax.rem(lax.div(seat, 1 << l), 2)
        return seat + (1 - 2 * bit) * (1 << l)

    def cols(owner, j, width):
        return pl.ds(pl.multiple_of((owner * kv_local + j) * width, width), width)

    def rows(n, r):
        return pl.ds(pl.multiple_of(n * block + r * t, t), t)

    anchor_rows = pl.ds((levels + 1) * block, anchors)

    def half_rows(which):
        return pl.ds(pl.multiple_of((levels + 1) * block + which * half, 16), half)

    def to_head(src, dst, send, recv, d):
        return pltpu.make_async_remote_copy(
            src_ref=src, dst_ref=dst, send_sem=send, recv_sem=recv,
            device_id={"head": peer(d)}, device_id_type=mesh_id)

    def to_level(src, dst, send, recv, l):
        return pltpu.make_async_remote_copy(
            src_ref=src, dst_ref=dst, send_sem=send, recv_sem=recv,
            device_id={"seq": partner(l)}, device_id_type=mesh_id)

    def own_copy(j, c):
        return pltpu.make_async_copy(
            sources[c].at[:, cols(me, j, HD)], kv.at[j, c, rows(0, me)], own_sem.at[j, c])

    def full_copy(c):
        return pltpu.make_async_copy(sources[c], full.at[c], full_sem.at[c])

    def own_q(j):
        return pltpu.make_async_copy(
            queries_ref.at[:, cols(me, j, wide)], qbuf.at[j, 0], own_q_sem.at[j])

    def send_kv(j, c, d):
        return to_head(
            sources[c].at[:, cols(peer(d), j, HD)], kv.at[j, c, rows(0, me)],
            x_send.at[j, c, d], x_recv.at[j, c, d], d)

    def came_kv(j, c, d):
        return to_head(
            sources[c].at[:, cols(me, j, HD)], kv.at[j, c, rows(0, peer(heads - d))],
            x_send.at[j, c, d], x_recv.at[j, c, d], d)

    def send_q(j, d):
        return to_head(
            queries_ref.at[:, cols(peer(d), j, wide)], qbuf.at[j, d],
            q_send.at[j, d], q_recv.at[j, d], d)

    def send_level(j, c, d, l):
        r = peer(heads - d)
        src = sources[c].at[:, cols(me, j, HD)] if d == 0 else kv.at[j, c, rows(0, r)]
        return to_level(
            src, kv.at[j, c, rows(l + 1, r)],
            lv_send.at[j, c, d, l], lv_recv.at[j, c, d, l], l)

    def level_came(j, c, d, l):
        r = peer(heads - d)
        return to_level(
            kv.at[j, c, rows(0, r)], kv.at[j, c, rows(l + 1, r)],
            lv_send.at[j, c, d, l], lv_recv.at[j, c, d, l], l)

    def send_core():
        return to_level(part.at[1 - mine], part_in, core_send, core_recv, 0)

    def send_part(d):
        return to_head(head_out.at[peer(d)], head_in.at[d], head_send.at[d], head_recv.at[d], d)

    def send_pair():
        return to_level(pair.at[1 - side], pair_in, pair_send, pair_recv, 1)

    def send_carry(i, l):
        return to_level(carry.at[i], carry_in.at[i], carry_send.at[i], carry_recv.at[i], l)

    def own_half(j):
        return pltpu.make_async_copy(
            carry.at[levels - 2, j], kv.at[j, mine, half_rows(side)], last_sem.at[j])

    def send_half(j):
        return to_level(
            carry.at[levels - 2, j], kv.at[j, mine, half_rows(side)],
            half_send.at[j], half_recv.at[j], 1)

    def half_came(j):
        return to_level(
            carry.at[levels - 2, j], kv.at[j, mine, half_rows(1 - side)],
            half_send.at[j], half_recv.at[j], 1)

    def send_last(j):
        return to_level(
            kv.at[j, mine, anchor_rows], kv.at[j, mine, anchor_rows],
            last_send.at[j], last_recv.at[j], 0)

    def last_came(j):
        return to_level(
            kv.at[j, mine, anchor_rows], kv.at[j, 1 - mine, anchor_rows],
            last_send.at[j], last_recv.at[j], 0)

    def out_cols(owner, j, g):
        return pl.ds(pl.multiple_of(((owner * kv_local + j) * group + g) * HD, HD), HD)

    def send_out(j, g, d):
        return to_head(
            obuf.at[j, d, g], out_ref.at[:, out_cols(me, j, g)],
            o_send.at[j, g, d], o_recv.at[j, g, d], heads - d)

    def came_out(j, g, d):
        return to_head(
            obuf.at[j, d, g], out_ref.at[:, out_cols(peer(d), j, g)],
            o_send.at[j, g, d], o_recv.at[j, g, d], heads - d)

    def small(i):
        src = (level_hbm, anchor_hbm, partners_hbm, places_hbm)[i]
        dst = (level_ref, anchor_ref, partners_ref, places_ref)[i]
        return pltpu.make_async_copy(src, dst, small_sem.at[i])

    barrier = pltpu.get_barrier_semaphore()
    for d in range(1, heads):
        pl.semaphore_signal(barrier, inc=1, device_id={"head": peer(d)}, device_id_type=mesh_id)
    for l in range(levels):
        pl.semaphore_signal(barrier, inc=1, device_id={"seq": partner(l)}, device_id_type=mesh_id)

    for c in range(2):
        full_copy(c).start()
    for i in range(4):
        small(i).start()
    for j in range(kv_local):
        for c in range(2):
            own_copy(j, c).start()
        own_q(j).start()
    pl.semaphore_wait(barrier, heads - 1 + levels)

    far = list(reversed(range(levels)))

    def push_kv(j):
        for d in range(1, heads):
            for c in range(2):
                send_kv(j, c, d).start()

    def push_levels(j, c, d):
        for l in far:
            send_level(j, c, d, l).start()

    push_kv(0)
    for c in range(2):
        push_levels(0, c, 0)

    small(3).wait()
    first = (seat * heads + me) * t
    places = places_ref[...] - first
    token = lax.broadcasted_iota(jnp.int32, (t, anchors), 0)
    selector = jnp.where(places == token, 1.0, 0.0).astype(bf16)
    for c in range(2):
        full_copy(c).wait()
        found = lax.dot_general(
            selector, full[c], (((0,), (0,)), ((), ())), preferred_element_type=jnp.float32)
        found = found.astype(bf16)
        for owner in range(heads):
            for j in range(kv_local):
                at = (owner * kv_local + j) * HD
                part[c, owner, j] = found[:, at:at + HD]
    send_core().start()
    send_core().wait_recv()
    for d in range(heads):
        head_out[d] = (
            part[mine, d].astype(jnp.float32) + part_in[d].astype(jnp.float32)).astype(bf16)
    for d in range(1, heads):
        send_part(d).start()
    for j in range(1, kv_local):
        push_kv(j)
        if j == kv_local - 2:
            for d in range(1, heads):
                send_q(0, d).start()
    for j in range(0 if kv_local < 3 else 1, kv_local):
        for d in range(1, heads):
            send_q(j, d).start()

    def wait_kv(j, c):
        own_copy(j, c).wait()
        for d in range(1, heads):
            came_kv(j, c, d).wait_recv()

    pending = [(0, c, d) for c in range(2) for d in range(1, heads)]
    for j in range(1, kv_local):
        pending += [(j, c, 0) for c in range(2)]
        pending += [(j, c, d) for c in range(2) for d in range(1, heads)]

    def push(count):
        for _ in range(min(count, len(pending))):
            j, c, d = pending.pop(0)
            if d == 0:
                own_copy(j, c).wait()
            else:
                came_kv(j, c, d).wait_recv()
            push_levels(j, c, d)

    for c in range(2):
        own_copy(0, c).wait()

    def fill_table():
        for i in range(3):
            small(i).wait()
        match = [[jnp.where(partners_ref[0, m] == partner(l), LOG2E, 0.0) for m in range(levels)]
                 for l in range(levels)]

        def fill(h, _):
            biases = [level_ref[m, h] for m in range(levels)]
            for l in range(levels):
                table[l, h] = sum(match[l][m] * biases[m] for m in range(levels))
            table[levels, h] = anchor_ref[h] * LOG2E
            return 0

        lax.fori_loop(0, kv_local * group, fill, 0)

    held = head_out[me].astype(jnp.float32)
    for d in range(1, heads):
        send_part(d).wait_recv()
        held = held + head_in[d].astype(jnp.float32)
    for which in range(2):
        pair[which] = held[:, which * half:(which + 1) * half].astype(bf16)
    send_pair().start()
    push(1)
    fill_table()
    send_pair().wait_recv()
    carry[0] = (pair[side].astype(jnp.float32) + pair_in[...].astype(jnp.float32)).astype(bf16)
    order = list(range(2, levels))
    for i, l in enumerate(order):
        send_carry(i, l).start()
        push(1)
        send_carry(i, l).wait_recv()
        carry[i + 1] = (
            carry[i].astype(jnp.float32) + carry_in[i].astype(jnp.float32)).astype(bf16)
    for j in range(kv_local):
        own_half(j).start()
        send_half(j).start()
    push(2)
    for j in range(kv_local):
        own_half(j).wait()
        half_came(j).wait_recv()
        send_last(j).start()
    push(len(pending))

    def answer(j, d, g):
        return attend(
            qbuf[j, d, :, g * HD:(g + 1) * HD],
            [kv[j, 0, n * block:(n + 1) * block] for n in range(levels + 1)]
            + [kv[j, 0, (levels + 1) * block:]],
            kv[j, 1],
            [jnp.float32(0.0)] + [table[l, j * group + g] for l in range(levels + 1)],
            scale,
        ).astype(bf16)

    def one(j, _):
        last_came(j).wait_recv()
        for l in range(levels):
            for c in range(2):
                for d in range(heads):
                    level_came(j, c, d, l).wait_recv()

        def remote(i, _):
            d = i + 1
            send_q(j, d).wait_recv()
            for g in range(group):
                obuf[j, d, g] = answer(j, d, g)
            for g in range(group):
                send_out(j, g, d).start()
            return 0

        lax.fori_loop(0, heads - 1, remote, 0)
        own_q(j).wait()
        for g in range(group):
            out_ref[:, out_cols(me, j, g)] = answer(j, 0, g)
        return 0

    lax.fori_loop(0, kv_local, one, 0)

    send_core().wait_send()
    send_pair().wait_send()
    for d in range(1, heads):
        send_part(d).wait_send()
    for i, l in enumerate(order):
        send_carry(i, l).wait_send()
    for j in range(kv_local):
        send_half(j).wait_send()
        send_last(j).wait_send()
        for c in range(2):
            for d in range(heads):
                for l in range(levels):
                    send_level(j, c, d, l).wait_send()
            for d in range(1, heads):
                send_kv(j, c, d).wait_send()
        for d in range(1, heads):
            send_q(j, d).wait_send()
        for g in range(group):
            for d in range(1, heads):
                send_out(j, g, d).wait_send()
                came_out(j, g, d).wait_recv()


def on_device(queries, keys, values, level_bias, anchor_bias, partners, anchor_positions):
    t = queries.shape[0]
    heads = lax.axis_size("head")
    levels = lax.axis_size("seq").bit_length() - 1
    kv_local = keys.shape[1] // HD // heads
    group = level_bias.shape[0] // kv_local
    anchors = anchor_positions.shape[0]
    vmem = pl.BlockSpec(memory_space=pltpu.VMEM)
    hbm = pl.BlockSpec(memory_space=pl.ANY)
    dma = pltpu.SemaphoreType.DMA
    anchor_shape = (kv_local, anchors, HD)
    half_shape = (kv_local, anchors // 2, HD)
    bf16 = jnp.bfloat16
    grant = (61 << 20) - 500_000 - queries.size * queries.dtype.itemsize
    return pl.pallas_call(
        functools.partial(kernel, heads, levels, kv_local, group),
        in_specs=[hbm] * 7,
        out_specs=vmem,
        out_shape=pltpu.VMEM(queries.shape, queries.dtype),
        scratch_shapes=[
            pltpu.SMEM(level_bias.shape[::-1], level_bias.dtype),
            pltpu.SMEM(anchor_bias.shape, anchor_bias.dtype),
            pltpu.SMEM(partners.shape, partners.dtype),
            pltpu.VMEM((1, anchors), anchor_positions.dtype),
            dma((4,)),
            pltpu.VMEM((kv_local, 2, (levels + 1) * heads * t + anchors, HD), bf16),
            pltpu.VMEM((kv_local, heads, t, group * HD), bf16),
            pltpu.VMEM((kv_local, heads, group, t, HD), bf16),
            pltpu.VMEM((2,) + keys.shape, bf16),
            pltpu.VMEM((2, heads) + anchor_shape, bf16),
            pltpu.VMEM((heads,) + anchor_shape, bf16),
            pltpu.VMEM((heads,) + anchor_shape, bf16),
            pltpu.VMEM((heads,) + anchor_shape, bf16),
            pltpu.VMEM((2,) + half_shape, bf16),
            pltpu.VMEM(half_shape, bf16),
            pltpu.VMEM((levels,) + half_shape, bf16),
            pltpu.VMEM((levels,) + half_shape, bf16),
            pltpu.SMEM((levels + 1, kv_local * group), jnp.float32),
            dma((kv_local, 2)), dma((2,)), dma((kv_local,)),
            dma((kv_local, 2, heads)), dma((kv_local, 2, heads)),
            dma((kv_local, heads)), dma((kv_local, heads)),
            dma((kv_local, group, heads)), dma((kv_local, group, heads)),
            dma((kv_local, 2, heads, levels)), dma((kv_local, 2, heads, levels)),
            dma, dma, dma((heads,)), dma((heads,)), dma, dma, dma((levels,)), dma((levels,)),
            dma((kv_local,)), dma((kv_local,)), dma((kv_local,)), dma((kv_local,)), dma((kv_local,)),
        ],
        compiler_params=pltpu.CompilerParams(
            vmem_limit_bytes=grant, collective_id=0, has_side_effects=True),
        name="attend",
    )(level_bias.T, anchor_bias, partners, anchor_positions[None, :], keys, values, queries)


def solution(mesh):
    in_specs = (
        P(("seq", "head"), None),
        P(("seq", "head"), None),
        P(("seq", "head"), None),
        P("head", None),
        P("head"),
        P("seq", None),
        P(),
    )
    out_specs = P(("seq", "head"), None)
    return jax.shard_map(
        on_device, mesh=mesh, in_specs=in_specs, out_specs=out_specs, check_vma=False
    )
```
